32 devices in a mesh: space: 2 (over x), expert: 16 (over z, y, core).
Axes of the slice: x: 2, y: 2, z: 4, core: 2. Of those that a mesh axis runs over, the one named last changes fastest.
Arguments:
- vertex_tiles: bfloat16 [4096, 512], P(('space', 'expert')), may hold values from -6 to 6
- cotangent: bfloat16 [4096, 512], P(('space', 'expert')), may hold values from -3 to 3
- frames: int32 [4096], P(('space', 'expert')), may hold values from 0 to 5
- expert_ids: int32 [4096, 2], P(('space', 'expert')), may hold values from 0 to 15, as said below
- gate_values: bfloat16 [4096, 2], P(('space', 'expert')), may hold values from 0.19921875 to 1
- w_in: bfloat16 [16, 512, 4096], P('expert', None, 'space'), may hold values from -0.25 to 0.25
- w_out: bfloat16 [16, 4096, 512], P('expert', 'space'), may hold values from -0.09375 to 0.09375
Outputs:
- d_tiles: bfloat16 [4096, 512], P(('space', 'expert'))
- d_gates: bfloat16 [4096, 2], P(('space', 'expert'))
- d_w_in: float32 [16, 512, 4096], P('expert', None, 'space')
- d_w_out: float32 [16, 4096, 512], P('expert', 'space')
The draws below stay inside these ranges and needn't reach their ends.
Inputs may be any that keep to these rules, and one draw needn't show every extreme that they name: `expert_ids`: in each device's aligned block of 128 tiles the two experts of a tile differ and no expert is named more than 20 times; one expert is named exactly 20 times in every block.
All inputs are finite; a program needn't handle non-finite values.
Results may differ from the reference program's by a relative error of at most 0.017.
Values may be sent and summed in bfloat16 or wider, within the bound.
A program may use at most 64 MiB of HBM per device.

```python
import math
import jax
import jax.numpy as jnp
from jax import lax

D = 512
FF = 4096
TOK_DEV = 128
E = 16
CAP = 20
FF_DEV = 2048
TOKENS = 4096


def draw_expert_ids(key, part):
    blocks = TOKENS // TOK_DEV
    slot_count = 2 * TOK_DEV
    hot_key, block_key = jax.random.split(jax.random.fold_in(key, 11))
    hottest = jax.random.randint(hot_key, (), 0, E)
    copies = jnp.repeat(jnp.arange(E, dtype=jnp.int32), CAP)

    def one_block(single_key):
        first_key, second_key, third_key = jax.random.split(single_key, 3)
        scores = jax.random.permutation(first_key, E * CAP).astype(jnp.int32)
        scores = jnp.where(copies == hottest, scores - E * CAP, scores)
        chosen = jnp.sort(copies[jnp.argsort(scores)[:slot_count]])
        paired = jnp.stack([chosen[:TOK_DEV], chosen[TOK_DEV:]], axis=1)
        paired = paired[jax.random.permutation(second_key, TOK_DEV)]
        flipped = jax.random.randint(third_key, (TOK_DEV, 1), 0, 2)
        return jnp.where(flipped == 1, paired[:, ::-1], paired)
    block_keys = jax.random.split(block_key, blocks)
    return jax.vmap(one_block)(block_keys).reshape(TOKENS, 2).astype(jnp.int32)


def place_ends(result, stream_key, low, top_value):
    index_at = [jax.random.randint(jax.random.fold_in(stream_key, axis), (), 0, length) for axis, length in enumerate(result.shape)]
    main_axis = result.shape.index(max(result.shape))
    beside = index_at[:main_axis] + [(index_at[main_axis] + 1) % result.shape[main_axis]] + index_at[main_axis + 1:]
    return result.at[tuple(index_at)].set(low).at[tuple(beside)].set(top_value)


def levels(own_key, extent, cuts, smallest, top_value):
    def one(axis_at, blocks):
        draws = jax.random.uniform(jax.random.fold_in(jax.random.fold_in(own_key, 6), axis_at), (blocks,), jnp.float32, smallest / len(cuts), top_value / len(cuts))
        return jnp.repeat(jnp.exp(draws), extent[axis_at] // blocks).reshape((-1,) + (1,) * (len(extent) - axis_at - 1))

    factor_of = one(*cuts[0])
    for cut in cuts[1:]:
        factor_of = factor_of * one(*cut)
    return factor_of


def bell_draw(rng, dims, spread, most, pieces=(), held_as=jnp.bfloat16):
    entries = spread * jax.random.normal(rng, dims, jnp.float32)
    if pieces:
        entries = entries * levels(rng, dims, pieces, -0.22, 0.18)
    return jnp.clip(entries, -most, most).astype(held_as)


def setup_inputs(seed: int = 0) -> dict:
    key_of = jax.random.split(jax.random.key(seed), 8)
    return {
        "vertex_tiles": bell_draw(key_of[0], (TOKENS, D), 1.0, 6.0, ((0, 32),)),
        "cotangent": bell_draw(key_of[1], (TOKENS, D), 0.5, 3.0, ((0, 32),)),
        "frames": place_ends(jax.random.randint(key_of[2], (TOKENS,), 0, 6), jax.random.fold_in(key_of[2], 1), 0, 5).astype(jnp.int32),
        "expert_ids": draw_expert_ids(jax.random.fold_in(key_of[7], 71), 0),
        "gate_values": jnp.clip(0.19921875 + 0.80078125 * jax.random.uniform(key_of[4], (TOKENS, 2), jnp.float32) ** levels(key_of[4], (TOKENS, 2), ((0, 32),), -0.2, 0.2), 0.19921875, 1.0).astype(jnp.bfloat16),
        "w_in": bell_draw(key_of[5], (E, D, FF), D ** -0.5, 0.25, ((0, 16), (2, 2))),
        "w_out": bell_draw(key_of[6], (E, FF, D), FF ** -0.5, 0.09375, ((0, 16), (1, 2))),
    }


def rotation_tables(frames, half_width):
    pair_index = jnp.arange(half_width, dtype=jnp.int32)
    frequency = (1 + pair_index % 3).astype(jnp.float32)
    angles = frames.astype(jnp.float32)[:, None] * frequency[None, :] * (math.pi / 3.0)
    return (jnp.cos(angles), jnp.sin(angles))

def turn_forward(values, cos_table, sin_table):
    half_width = cos_table.shape[1]
    first_half = values[:, :half_width].astype(jnp.float32)
    second_half = values[:, half_width:].astype(jnp.float32)
    return jnp.concatenate([cos_table * first_half - sin_table * second_half, sin_table * first_half + cos_table * second_half], axis=1)

def turn_back(values, cos_table, sin_table):
    half_width = cos_table.shape[1]
    first_half = values[:, :half_width]
    second_half = values[:, half_width:]
    return jnp.concatenate([cos_table * first_half + sin_table * second_half, cos_table * second_half - sin_table * first_half], axis=1)

def gelu_pair(hidden):
    gelu_scale = math.sqrt(2.0 / math.pi)
    inner_arg = gelu_scale * (hidden + 0.044715 * hidden * hidden * hidden)
    tangent_h = jnp.tanh(inner_arg)
    activated = 0.5 * hidden * (1.0 + tangent_h)
    slope_term = 0.5 * (1.0 + tangent_h) + 0.5 * hidden * (1.0 - tangent_h * tangent_h) * gelu_scale * (1.0 + 0.134145 * hidden * hidden)
    return (activated, slope_term)

def expert_terms(block_items):
    x_rows, dy_rows, g_rows, first_weight, second_weight = block_items
    row_count = x_rows.shape[0]
    groups = FF // FF_DEV
    hidden = jnp.dot(x_rows, first_weight, preferred_element_type=jnp.float32)
    activated, slope_term = gelu_pair(hidden)
    active = activated.astype(jnp.bfloat16)
    back = jnp.dot(dy_rows, second_weight.T, preferred_element_type=jnp.float32)
    gate_piece = lax.optimization_barrier(jnp.sum((back * active.astype(jnp.float32)).reshape(row_count, groups, FF_DEV), axis=2)).astype(jnp.bfloat16)
    gate_piece = lax.optimization_barrier(gate_piece)
    gate_grad = lax.optimization_barrier(jnp.sum(gate_piece.astype(jnp.float32), axis=1)).astype(jnp.bfloat16)
    gate_col = g_rows.astype(jnp.float32)[:, None]
    scaled = (gate_col * dy_rows.astype(jnp.float32)).astype(jnp.bfloat16)
    pre = (gate_col * back * slope_term).astype(jnp.bfloat16)
    d_first = jnp.dot(x_rows.T, pre, preferred_element_type=jnp.float32)
    d_second = jnp.dot(active.T, scaled, preferred_element_type=jnp.float32)
    row_piece = jnp.einsum('rgf,dgf->grd', pre.astype(jnp.float32).reshape(row_count, groups, FF_DEV), first_weight.astype(jnp.float32).reshape(D, groups, FF_DEV)).astype(jnp.bfloat16)
    row_piece = lax.optimization_barrier(row_piece)
    slot_grad = lax.optimization_barrier(jnp.sum(row_piece.astype(jnp.float32), axis=0)).astype(jnp.bfloat16)
    return (slot_grad, gate_grad, d_first, d_second)

def reference(vertex_tiles, cotangent, frames, expert_ids, gate_values, w_in, w_out):
    tile_count = vertex_tiles.shape[0]
    feature_dim = vertex_tiles.shape[1]
    half_width = feature_dim // 2
    blocks = tile_count // TOK_DEV
    cos_table, sin_table = rotation_tables(frames, half_width)
    rotated = turn_forward(vertex_tiles, cos_table, sin_table).astype(jnp.bfloat16)
    turned = turn_forward(cotangent, cos_table, sin_table).astype(jnp.bfloat16)
    grouped = expert_ids.reshape(blocks, 2 * TOK_DEV)
    onehot = (grouped[:, :, None] == jnp.arange(E, dtype=jnp.int32)[None, None, :]).astype(jnp.int32)
    slot_rank = lax.optimization_barrier(jnp.sum(jnp.cumsum(onehot, axis=1) * onehot, axis=2)) - 1
    position = (jnp.arange(blocks, dtype=jnp.int32)[:, None] * CAP + slot_rank).reshape(-1).astype(jnp.int32)
    flat_ids = expert_ids.reshape(-1).astype(jnp.int32)
    row_total = blocks * CAP
    slot_x = jnp.repeat(rotated, 2, axis=0)
    slot_dy = jnp.repeat(turned, 2, axis=0)
    buffer_x = jnp.zeros((E, row_total, feature_dim), jnp.bfloat16).at[flat_ids, position].set(slot_x)
    buffer_dy = jnp.zeros((E, row_total, feature_dim), jnp.bfloat16).at[flat_ids, position].set(slot_dy)
    buffer_g = jnp.zeros((E, row_total), jnp.bfloat16).at[flat_ids, position].set(gate_values.reshape(-1))
    slot_grads, gate_grads, d_w_in, d_w_out = lax.map(expert_terms, (buffer_x, buffer_dy, buffer_g, w_in, w_out))
    picked = slot_grads[flat_ids, position].astype(jnp.float32).reshape(tile_count, 2, feature_dim)
    total = picked[:, 0, :] + picked[:, 1, :]
    d_tiles = turn_back(total, cos_table, sin_table).astype(jnp.bfloat16)
    d_gates = gate_grads[flat_ids, position].reshape(tile_count, 2)
    return (d_tiles, d_gates, d_w_in, d_w_out)
```

```python
import contextlib
import math

import jax
import jax.numpy as jnp
from jax import lax
from jax.experimental import pallas as pl
from jax.experimental.pallas import tpu as pltpu
from jax.sharding import PartitionSpec as P


def rotation_tables(frames, half_width):
    pair_index = jnp.arange(half_width, dtype=jnp.int32)
    frequency = (1 + pair_index % 3).astype(jnp.float32)
    angles = frames.astype(jnp.float32)[:, None] * frequency[None, :] * (math.pi / 3.0)
    return (jnp.cos(angles), jnp.sin(angles))


def turn_forward(values, cos_table, sin_table):
    half_width = cos_table.shape[1]
    first_half = values[:, :half_width].astype(jnp.float32)
    second_half = values[:, half_width:].astype(jnp.float32)
    return jnp.concatenate(
        [
            cos_table * first_half - sin_table * second_half,
            sin_table * first_half + cos_table * second_half,
        ],
        axis=1,
    )


def turn_back(values, cos_table, sin_table):
    half_width = cos_table.shape[1]
    first_half = values[:, :half_width]
    second_half = values[:, half_width:]
    return jnp.concatenate(
        [
            cos_table * first_half + sin_table * second_half,
            cos_table * second_half - sin_table * first_half,
        ],
        axis=1,
    )


def gelu_pair(hidden):
    gelu_scale = math.sqrt(2.0 / math.pi)
    inner_arg = gelu_scale * (hidden + 0.044715 * hidden * hidden * hidden)
    tangent_h = jnp.tanh(inner_arg)
    activated = 0.5 * hidden * (1.0 + tangent_h)
    slope_term = 0.5 * (1.0 + tangent_h) + 0.5 * hidden * (
        1.0 - tangent_h * tangent_h
    ) * gelu_scale * (1.0 + 0.134145 * hidden * hidden)
    return (activated, slope_term)


def slot_targets(route_ids, capacity, expert_count):
    flat_ids = route_ids.reshape(-1)
    onehot = (flat_ids[:, None] == jnp.arange(expert_count, dtype=jnp.int32)[None, :]).astype(
        jnp.int32
    )
    slot_rank = jnp.sum(jnp.cumsum(onehot, axis=0) * onehot, axis=1) - 1
    return flat_ids * capacity + slot_rank


def fill_buffer(rows_x, rows_dy, gate_rows, targets, slots_total):
    positions = jnp.arange(slots_total, dtype=jnp.int32)
    matches = (positions[:, None] == targets[None, :]).astype(jnp.int32)
    filled = jnp.sum(matches, axis=1)
    source = jnp.sum(matches * jnp.arange(targets.shape[0], dtype=jnp.int32)[None, :], axis=1)
    token_index = source // 2
    occupied = filled > 0
    nothing = jnp.zeros((), jnp.bfloat16)
    buffer_x = jnp.where(occupied[:, None], jnp.take(rows_x, token_index, axis=0), nothing)
    buffer_dy = jnp.where(occupied[:, None], jnp.take(rows_dy, token_index, axis=0), nothing)
    buffer_g = jnp.where(occupied, jnp.take(gate_rows.reshape(-1), source, axis=0), nothing)
    return (buffer_x, buffer_dy, buffer_g)


def block_terms(rows_x, rows_dy, rows_g, first_weight, second_weight):
    hidden = jnp.dot(rows_x, first_weight, preferred_element_type=jnp.float32)
    activated, slope_term = gelu_pair(hidden)
    active = activated.astype(jnp.bfloat16)
    back = jnp.einsum("rd,fd->rf", rows_dy, second_weight, preferred_element_type=jnp.float32)
    gate_part = jnp.sum(back * active.astype(jnp.float32), axis=1)
    gate_col = rows_g.astype(jnp.float32)[:, None]
    scaled = (gate_col * rows_dy.astype(jnp.float32)).astype(jnp.bfloat16)
    pre = (gate_col * back * slope_term).astype(jnp.bfloat16)
    d_first = jnp.einsum("rd,rf->df", rows_x, pre, preferred_element_type=jnp.float32)
    d_second = jnp.einsum("rf,rd->fd", active, scaled, preferred_element_type=jnp.float32)
    row_part = jnp.einsum("rf,df->rd", pre, first_weight, preferred_element_type=jnp.float32)
    return (d_first, d_second, row_part, gate_part)


def run_blocks(blocks_x, blocks_dy, blocks_g, first_weight, second_weight):
    feature_dim = blocks_x.shape[2]

    def scan_step(carried, block_items):
        d_first, d_second, row_part, gate_part = block_terms(
            block_items[0], block_items[1], block_items[2], first_weight, second_weight
        )
        return ((carried[0] + d_first, carried[1] + d_second), (row_part, gate_part))

    start_value = (
        jnp.zeros(first_weight.shape, jnp.float32),
        jnp.zeros(second_weight.shape, jnp.float32),
    )
    sums, stacked = lax.scan(scan_step, start_value, (blocks_x, blocks_dy, blocks_g))
    return (sums[0], sums[1], stacked[0].reshape(-1, feature_dim), stacked[1].reshape(-1))


def on_device(vertex_tiles, cotangent, frames, expert_ids, gate_values, w_in, w_out):
    tile_count = vertex_tiles.shape[0]
    feature_dim = vertex_tiles.shape[1]
    expert_count = lax.axis_size("expert")
    space_count = lax.axis_size("space")
    capacity = 5 * tile_count // (2 * expert_count)
    slots_total = expert_count * capacity
    cos_table, sin_table = rotation_tables(frames, feature_dim // 2)
    rotated = turn_forward(vertex_tiles, cos_table, sin_table).astype(jnp.bfloat16)
    turned = turn_forward(cotangent, cos_table, sin_table).astype(jnp.bfloat16)
    first_weight = w_in[0]
    second_weight = w_out[0]
    own_targets = slot_targets(expert_ids, capacity, expert_count)
    group_x, group_dy, group_g = (
        lax.all_gather(rotated, "space", axis=0, tiled=True),
        lax.all_gather(turned, "space", axis=0, tiled=True),
        lax.all_gather(gate_values, "space", axis=0, tiled=True),
    )
    group_ids = lax.all_gather(expert_ids, "space", axis=0, tiled=True)

    def fill_group(rows_x, rows_dy, gate_rows, route_ids):
        return fill_buffer(
            rows_x, rows_dy, gate_rows, slot_targets(route_ids, capacity, expert_count), slots_total
        )

    buffer_x, buffer_dy, buffer_g = jax.vmap(fill_group)(
        group_x.reshape(space_count, tile_count, feature_dim),
        group_dy.reshape(space_count, tile_count, feature_dim),
        group_g.reshape(space_count, tile_count, 2),
        group_ids.reshape(space_count, tile_count, 2),
    )
    recv_x, recv_dy, recv_g = (
        lax.all_to_all(
            buffer_x.reshape(space_count, expert_count, capacity, feature_dim),
            "expert",
            split_axis=1,
            concat_axis=1,
            tiled=True,
        ),
        lax.all_to_all(
            buffer_dy.reshape(space_count, expert_count, capacity, feature_dim),
            "expert",
            split_axis=1,
            concat_axis=1,
            tiled=True,
        ),
        lax.all_to_all(
            buffer_g.reshape(space_count, expert_count, capacity),
            "expert",
            split_axis=1,
            concat_axis=1,
            tiled=True,
        ),
    )
    d_first, d_second, row_parts, gate_parts = run_blocks(
        recv_x.reshape(space_count, slots_total, feature_dim),
        recv_dy.reshape(space_count, slots_total, feature_dim),
        recv_g.reshape(space_count, slots_total),
        first_weight,
        second_weight,
    )
    summed_rows, summed_gates = (
        lax.psum_scatter(
            row_parts.astype(jnp.bfloat16), "space", scatter_dimension=0, tiled=True
        ).astype(jnp.float32),
        lax.psum_scatter(
            gate_parts.astype(jnp.bfloat16), "space", scatter_dimension=0, tiled=True
        ).astype(jnp.float32),
    )
    back_rows = summed_rows.astype(jnp.bfloat16).reshape(expert_count, capacity, feature_dim)
    back_gates = summed_gates.astype(jnp.bfloat16).reshape(expert_count, capacity)
    home_rows, home_gates = (
        lax.all_to_all(back_rows, "expert", split_axis=0, concat_axis=0, tiled=True),
        lax.all_to_all(back_gates, "expert", split_axis=0, concat_axis=0, tiled=True),
    )
    picked = jnp.take(home_rows.reshape(slots_total, feature_dim), own_targets, axis=0).astype(
        jnp.float32
    )
    picked = picked.reshape(tile_count, 2, feature_dim)
    total = picked[:, 0, :] + picked[:, 1, :]
    d_tiles = turn_back(total, cos_table, sin_table).astype(jnp.bfloat16)
    d_gates = jnp.take(home_gates.reshape(slots_total), own_targets, axis=0).reshape(tile_count, 2)
    return (d_tiles, d_gates, d_first[None], d_second[None])


MESH = pl.DeviceIdType.MESH
BF = jnp.bfloat16
F32 = jnp.float32
LEAD = 16
REST = 4
SELF = 12
CHUNKS = ((0, 4), (4, 8), (8, 12), (12, 16))
DIRECT = 8
SENDS = (13, 14, 15, 0, 1, 2, 3, 4, 5, 6, 7, 8, 9, 10, 11)
FIRST = (13, 14, 0, 1, 2, 3, 15, 4)
DURING = ((6, 5, 7), (8, 9, 10, 11), (), ())


def mark(name):
    return contextlib.nullcontext()


def mm(a, b, ca, cb):
    return lax.dot_general(a, b, (((ca,), (cb,)), ((), ())), preferred_element_type=F32)


def iota(shape, axis):
    return lax.broadcasted_iota(jnp.int32, shape, axis)


def by_quarter(quarter, pieces):
    low = jnp.where(quarter == 0, pieces[0], pieces[1])
    high = jnp.where(quarter == 2, pieces[2], pieces[3])
    return jnp.where(quarter < 2, low, high)


def fused(
    tiles_h, cotan_h, frames_h, ids_h, gates_h, w_in, w_out,
    d_tiles, d_gates, d_first, d_second,
    x_all, sc_all, act_all, pre_all,
    own_gate, far_gate, near_gate, out_gate, home_gate,
    send, recv, own_piece, far_piece, near_in, home_out, home, pick_m, pick_t, rows_acc,
    w1, w2, tiles, cotan, frames_t, ids_t, gates_t,
    sem_w, sem_self, s1, r1, s2, r2, s3, r3, s4, r4, s5, r5, s6, r6,
):
    space = lax.axis_index("space")
    me = lax.axis_index("expert")
    zed, low = me // 4, me % 4
    slots = lax.axis_size("expert")
    other = 1 - space
    count, width = tiles_h.shape
    half = width // 2
    quarter_w = width // 4
    hidden_n = w1.shape[1]

    def flip(value, bits):
        if bits == 1:
            return value + 1 - 2 * lax.rem(value, 2)
        return (value, value, lax.rem(value + 2, 4), 3 - value)[bits]

    def peer(s):
        if s >= SELF:
            return flip(zed, 0) * 4 + flip(low, s - SELF)
        return flip(zed, (1, 3, 2)[s % 3]) * 4 + flip(low, s // 3)

    load1 = pltpu.make_async_copy(w_in.at[0], w1, sem_w.at[0])
    load2 = pltpu.make_async_copy(w_out.at[0], w2, sem_w.at[1])
    small = [
        pltpu.make_async_copy(src, dst, sem_w.at[2 + n])
        for n, (src, dst) in enumerate(
            (
                (ids_h, ids_t), (frames_h, frames_t), (gates_h, gates_t),
                (tiles_h, tiles), (cotan_h, cotan),
            )
        )
    ]
    for copy in small:
        copy.start()

    barrier = pltpu.get_barrier_semaphore()
    peers = [s for s in range(slots) if s != SELF]
    for s in peers:
        pl.semaphore_signal(barrier, inc=1, device_id=(space, peer(s)), device_id_type=MESH)
    for s in range(DIRECT, slots):
        pl.semaphore_signal(
            barrier, inc=1, device_id=(other, peer(s)), device_id_type=MESH
        )

    load1.start()
    load2.start()
    with mark("small"):
        for copy in small:
            copy.wait()
    ids = ids_t[...]
    rel = ids ^ me
    near, plane = rel & 3, (rel >> 2) ^ (rel >> 3)
    rel = jnp.where(plane == 0, SELF + near, 3 * near + plane - 1)
    upper = (iota((count, count), 0) < iota((count, count), 1)).astype(BF)
    hits = [(iota((slots, count), 0) == rel[k : k + 1, :]).astype(F32) for k in range(2)]
    before = mm(jnp.concatenate(hits, axis=0).astype(BF), upper, 1, 0)
    first_total = jnp.sum(hits[0], axis=1, keepdims=True)
    before = (before[:slots], before[slots:] + first_total)
    rows = slots * LEAD
    row_id = iota((rows, count), 0)
    row_tail = (row_id >> 4) * REST + (row_id & 3)
    ranks = []
    for k in range(2):
        rank = jnp.sum(before[k] * hits[k], axis=0, keepdims=True).astype(jnp.int32)
        ranks.append(rank)
        where = rel[k : k + 1, :]
        code_m = jnp.where(rank < LEAD, where * LEAD + rank, -1)
        code_t = jnp.where(rank >= LEAD, where * REST + rank - LEAD, -1)
        pick_m[k] = (row_id == code_m).astype(F32).astype(BF)
        pick_t[k] = (row_tail == code_t).astype(F32).astype(BF)

    diagonal = iota((count, count), 0) == iota((count, count), 1)
    frame = jnp.sum(jnp.where(diagonal, frames_t[...].astype(F32), 0.0), axis=1, keepdims=True)
    frequency = (1 + lax.rem(iota((1, half), 1), 3)).astype(F32)
    sixths = frequency * (frame - 6.0 * jnp.floor(frame * (1.0 / 6.0) + 0.01))
    sixths = sixths - 6.0 * jnp.floor(sixths * (1.0 / 6.0) + 0.01)
    folded = jnp.abs(sixths - 3.0)
    cos_v = jnp.where(
        folded > 2.5, 1.0, jnp.where(folded > 1.5, 0.5, jnp.where(folded > 0.5, -0.5, -1.0))
    )
    side = math.sqrt(3.0) / 2.0
    sin_v = jnp.where(
        (folded > 2.5) | (folded < 0.5), 0.0, jnp.where(sixths < 3.0, side, -side)
    )

    def turn(ref):
        u = ref[:, :half].astype(F32)
        v = ref[:, half:].astype(F32)
        return jnp.concatenate(
            [cos_v * u - sin_v * v, sin_v * u + cos_v * v], axis=1
        ).astype(BF)

    rotated = turn(tiles)
    turned = turn(cotan)
    g0 = gates_t[0:1, :].astype(F32)
    g1 = gates_t[1:2, :].astype(F32)

    def weighed(pick):
        return (pick[0].astype(F32) * g0 + pick[1].astype(F32) * g1).astype(BF)

    quarter = (iota((rows, 1), 0) >> 2) & 3
    send[:, :, 0:width] = (
        mm(pick_m[0] + pick_m[1], rotated, 1, 0).astype(BF).reshape(slots, LEAD, width)
    )
    send[:, :, width : 2 * width] = (
        mm(weighed(pick_m), turned, 1, 0).astype(BF).reshape(slots, LEAD, width)
    )
    tail_x = mm(pick_t[0] + pick_t[1], rotated, 1, 0)
    tail_y = mm(weighed(pick_t), turned, 1, 0)
    send[:, :, 2 * width :] = (
        by_quarter(
            quarter, (tail_x[:, :half], tail_x[:, half:], tail_y[:, :half], tail_y[:, half:])
        )
        .astype(BF)
        .reshape(slots, LEAD, half)
    )
    with mark("barrier_wait"):
        pl.semaphore_wait(barrier, 2 * slots - 1 - DIRECT)

    def remote(src, dst, a, b, who):
        return pltpu.make_async_remote_copy(
            src_ref=src, dst_ref=dst, send_sem=a, recv_sem=b, device_id=who, device_id_type=MESH
        )

    out_copy, relay_copy, piece_copy, home_copy = {}, {}, {}, {}
    piece_gate, home_gates, far_gates = {}, {}, {}
    self_copy = pltpu.make_async_copy(send.at[SELF], recv.at[0, SELF], sem_self)
    self_copy.start()
    relay_copy[SELF] = remote(
        send.at[SELF], recv.at[1, SELF], s2.at[SELF], r2.at[SELF], (other, me)
    )
    relay_copy[SELF].start()
    for s in SENDS:
        out_copy[s] = remote(send.at[s], recv.at[0, s], s1.at[s], r1.at[s], (space, peer(s)))
        out_copy[s].start()

    consts = {}
    for lo, hi in CHUNKS:
        block, rest = 2 * (hi - lo) * LEAD, 2 * (hi - lo) * REST
        if block in consts:
            continue
        spread_q = (iota((block, 1), 0) >> 2) & 3
        tall_r = iota((block, rest), 0)
        grow = (tall_r >> 4) * REST + (tall_r & 3) == iota((block, rest), 1)
        flat_c = iota((rest, block), 1)
        same = (flat_c >> 4) * REST + (flat_c & 3) == iota((rest, block), 0)
        pulls = [
            (same & (((flat_c >> 2) & 3) == q)).astype(F32).astype(BF) for q in range(4)
        ]
        consts[block] = (spread_q, grow.astype(F32).astype(BF), pulls)
    gelu_scale = math.sqrt(2.0 / math.pi)
    step_w = 512

    def relay(s):
        with mark("arrive%d" % s):
            out_copy[s].wait_recv()
        relay_copy[s] = remote(
            recv.at[0, s], recv.at[1, s], s2.at[s], r2.at[s], (other, me)
        )
        relay_copy[s].start()

    def work(c):
        lo, hi = CHUNKS[c]
        n = hi - lo
        block, rest = 2 * n * LEAD, 2 * n * REST
        chunk = block + rest
        spread_q, grow, pulls = consts[block]
        with mark("relayed%d" % c):
            for s in range(lo, hi):
                relay_copy[s].wait_recv()
        base = 2 * lo * (LEAD + REST)
        span = slice(lo, hi)
        x_all[base : base + block, :] = recv[:, span, :, 0:width].reshape(block, width)
        sc_all[base : base + block, :] = recv[:, span, :, width : 2 * width].reshape(block, width)
        tail = recv[:, span, :, 2 * width :].reshape(block, half)
        parts = [mm(pull, tail, 1, 0).astype(BF) for pull in pulls]
        x_all[base + block : base + chunk, :] = jnp.concatenate(parts[:2], axis=1)
        sc_all[base + block : base + chunk, :] = jnp.concatenate(parts[2:], axis=1)
        x_c = x_all[base : base + chunk, :]
        y_c = sc_all[base : base + chunk, :]
        acc = rows_acc.at[0:chunk]
        acc[...] = jnp.zeros((chunk, width), F32)

        def tile(f, gate):
            cols = pl.ds(f * step_w, step_w)
            w_a = w1[:, cols]
            h = mm(x_c, w_a, 1, 0)
            back = mm(y_c, w2[cols, :], 1, 1)
            sq = h * h
            t = jnp.tanh(gelu_scale * (h + 0.044715 * h * sq))
            up = 0.5 * (1.0 + t)
            active = (h * up).astype(BF)
            slope = up + 0.5 * h * (1.0 - t * t) * (gelu_scale + (gelu_scale * 0.134145) * sq)
            pre = (back * slope).astype(BF)
            act_all[base : base + chunk, cols] = active
            pre_all[base : base + chunk, cols] = pre
            acc[...] += mm(pre, w_a, 1, 1)
            return gate + jnp.sum(back * active.astype(F32), axis=1, keepdims=True)

        gate = jnp.zeros((chunk, 1), F32)
        for f in range(hidden_n // step_w):
            gate = tile(f, gate)
            for s in DURING[c][f : f + 1] if f < hidden_n // step_w - 1 else DURING[c][f:]:
                relay(s)
        main = rows_acc[0:block, :].astype(BF)
        wide = mm(grow, rows_acc[block:chunk, :].astype(BF), 1, 0)
        packed = by_quarter(
            spread_q, [wide[:, q * quarter_w : (q + 1) * quarter_w] for q in range(4)]
        ).astype(BF)
        gate_b = jnp.broadcast_to(gate.astype(BF).astype(F32), (chunk, 128))
        lane = iota((block, 128), 1)
        gate_m = jnp.where(lane == (iota((block, 128), 0) & (LEAD - 1)), gate_b[:block], 0.0)
        lane = iota((rest, 128), 1)
        gate_r = jnp.where(
            lane == LEAD + (iota((rest, 128), 0) & (REST - 1)), gate_b[block:], 0.0
        )
        gates = jnp.sum(gate_m.reshape(2 * n, LEAD, 128), axis=1) + jnp.sum(
            gate_r.reshape(2 * n, REST, 128), axis=1
        )
        for i in range(n):
            own_gate[lo + i] = gates[i : i + 1]
            far_gate[lo + i] = gates[n + i : n + i + 1]
        both = jnp.concatenate([main, packed], axis=1).reshape(2, n, LEAD, -1)
        far_piece[span] = both[1]
        own_piece[span] = both[0]
        if lo >= DIRECT:
            for s in range(lo, hi):
                there, here = (other, peer(s)), (space, peer(s))
                piece_copy[s] = remote(far_piece.at[s], near_in.at[s], s3.at[s], r3.at[s], there)
                piece_copy[s].start()
                far_gates[s] = remote(far_gate.at[s], near_gate.at[s], s5.at[s], r5.at[s], there)
                far_gates[s].start()
                if s == SELF:
                    home[s] = own_piece[s]
                    home_gate[s] = own_gate[s]
                    continue
                home_copy[s] = remote(own_piece.at[s], home.at[s], s4.at[s], r4.at[s], here)
                home_copy[s].start()
                home_gates[s] = remote(own_gate.at[s], home_gate.at[s], s6.at[s], r6.at[s], here)
                home_gates[s].start()
            return
        piece_gate[c] = remote(
            far_gate.at[pl.ds(lo, n)], near_gate.at[pl.ds(lo, n)],
            s5.at[c], r5.at[c], (other, me),
        )
        piece_gate[c].start()
        for s in range(lo, hi):
            piece_copy[s] = remote(
                far_piece.at[s], near_in.at[s], s3.at[s], r3.at[s], (other, me)
            )
            piece_copy[s].start()

    def finish(c):
        piece_gate[c].wait_recv()
        for s in range(*CHUNKS[c]):
            piece_copy[s].wait_recv()
            summed = (own_piece[s].astype(F32) + near_in[s].astype(F32)).astype(BF)
            gate = (own_gate[s] + near_gate[s]).astype(BF).astype(F32)
            out_gate[s] = gate
            home_gates[s] = remote(
                out_gate.at[s], home_gate.at[s], s6.at[s], r6.at[s], (space, peer(s))
            )
            home_gates[s].start()
            home_out[s] = summed
            home_copy[s] = remote(
                home_out.at[s], home.at[s], s4.at[s], r4.at[s], (space, peer(s))
            )
            home_copy[s].start()

    grad_w = 1024

    def first_tile(f, carry):
        cols = pl.ds(pl.multiple_of(f * grad_w, grad_w), grad_w)
        d_first[:, cols] = mm(x_all[...], pre_all[:, cols], 0, 0)
        return carry

    def second_tile(f, carry):
        cols = pl.ds(pl.multiple_of(f * grad_w, grad_w), grad_w)
        d_second[cols, :] = mm(act_all[:, cols], sc_all[...], 0, 0)
        return carry

    for s in FIRST:
        relay(s)
    self_copy.wait()
    load1.wait()
    load2.wait()
    for c in range(len(CHUNKS)):
        with mark("work%d" % c):
            work(c)
        if 0 < c and CHUNKS[c - 1][0] < DIRECT:
            with mark("finish%d" % (c - 1)):
                finish(c - 1)
    with mark("first"):
        lax.fori_loop(0, hidden_n // grad_w, first_tile, 0)
    with mark("second"):
        lax.fori_loop(0, hidden_n // grad_w, second_tile, 0)
    with mark("homewait"):
        for s in peers:
            home_copy[s].wait_recv()
            home_gates[s].wait_recv()
        for s in range(DIRECT, slots):
            piece_copy[s].wait_recv()
            far_gates[s].wait_recv()
    ends = slice(DIRECT, slots)
    home[ends] = (home[ends].astype(F32) + near_in[ends].astype(F32)).astype(BF)
    home_gate[ends] = (home_gate[ends] + near_gate[ends]).astype(BF).astype(F32)

    lead = home[:, :, 0:width].reshape(rows, width)
    packed = home[:, :, width : width + quarter_w].reshape(rows, quarter_w)
    nothing = jnp.zeros((), BF)
    spread = jnp.concatenate([jnp.where(quarter == q, packed, nothing) for q in range(4)], axis=1)
    total = mm(pick_m[0] + pick_m[1], lead, 0, 0) + mm(pick_t[0] + pick_t[1], spread, 0, 0)
    a, b = total[:, :half], total[:, half:]
    d_tiles[...] = jnp.concatenate(
        [cos_v * a + sin_v * b, cos_v * b - sin_v * a], axis=1
    ).astype(BF)
    gate_rows = home_gate[...].reshape(slots, 128).astype(BF)
    for k in range(2):
        got = mm(gate_rows, hits[k].astype(BF), 0, 0)
        row = jnp.sum(jnp.where(iota((128, count), 0) == ranks[k], got, 0.0), axis=0, keepdims=True)
        d_gates[k : k + 1, :] = (row / gates_t[k : k + 1, :].astype(F32)).astype(BF)

    for s in range(slots):
        if s != SELF:
            out_copy[s].wait_send()
            home_copy[s].wait_send()
            home_gates[s].wait_send()
        relay_copy[s].wait_send()
        piece_copy[s].wait_send()
    for s in range(DIRECT, slots):
        far_gates[s].wait_send()
    for c in piece_gate:
        piece_gate[c].wait_send()


def write_out(*refs):
    held, outs, sem = refs[:4], refs[4:8], refs[8]
    copies = [pltpu.make_async_copy(held[n], outs[n], sem.at[n]) for n in range(4)]
    for copy in copies:
        copy.start()
    for copy in copies:
        copy.wait()


def on_device_fused(vertex_tiles, cotangent, frames, expert_ids, gate_values, w_in, w_out):
    count, width = vertex_tiles.shape
    hidden_n = w_in.shape[2]
    slots = lax.axis_size("expert")
    rows = 2 * slots * (LEAD + REST)
    most = max(hi - lo for lo, hi in CHUNKS)
    block_w = 2 * width + width // 2
    piece_w = width + width // 4
    vmem = pl.BlockSpec(memory_space=pltpu.VMEM)
    hbm = pl.BlockSpec(memory_space=pltpu.HBM)
    dma = pltpu.SemaphoreType.DMA
    shape = jax.ShapeDtypeStruct
    row = pltpu.VMEM((slots, 1, 128), F32)
    d_tiles, d_gates, d_first, d_second = pl.pallas_call(
        fused,
        out_shape=(
            shape((count, width), BF),
            shape((2, count), BF),
            shape((width, hidden_n), F32),
            shape((hidden_n, width), F32),
        ),
        in_specs=[hbm] * 7,
        out_specs=[vmem] * 4,
        scratch_shapes=[
            pltpu.VMEM((rows, width), BF),
            pltpu.VMEM((rows, width), BF),
            pltpu.VMEM((rows, hidden_n), BF),
            pltpu.VMEM((rows, hidden_n), BF),
            row, row, row, row, row,
            pltpu.VMEM((slots, LEAD, block_w), BF),
            pltpu.VMEM((2, slots, LEAD, block_w), BF),
            pltpu.VMEM((slots, LEAD, piece_w), BF),
            pltpu.VMEM((slots, LEAD, piece_w), BF),
            pltpu.VMEM((slots, LEAD, piece_w), BF),
            pltpu.VMEM((slots, LEAD, piece_w), BF),
            pltpu.VMEM((slots, LEAD, piece_w), BF),
            pltpu.VMEM((2, slots * LEAD, count), BF),
            pltpu.VMEM((2, slots * LEAD, count), BF),
            pltpu.VMEM((2 * most * (LEAD + REST), width), F32),
            pltpu.VMEM((width, hidden_n), BF),
            pltpu.VMEM((hidden_n, width), BF),
            pltpu.VMEM((count, width), BF),
            pltpu.VMEM((count, width), BF),
            pltpu.VMEM((1, count), jnp.int32),
            pltpu.VMEM((2, count), jnp.int32),
            pltpu.VMEM((2, count), BF),
            dma((7,)),
            dma(()),
        ]
        + [dma((slots,))] * 12,
        compiler_params=pltpu.CompilerParams(
            collective_id=0, has_side_effects=True, vmem_limit_bytes=36 * 1024 * 1024
        ),
    )(
        *[
            pltpu.with_memory_space_constraint(a, pltpu.HBM)
            for a in (
                vertex_tiles, cotangent, frames[None], expert_ids.T, gate_values.T, w_in, w_out
            )
        ]
    )
    results = (d_tiles, d_gates, d_first, d_second)
    d_tiles, d_gates, d_first, d_second = pl.pallas_call(
        write_out,
        out_shape=tuple(shape(a.shape, a.dtype) for a in results),
        in_specs=[vmem] * 4,
        out_specs=[hbm] * 4,
        scratch_shapes=[dma((4,))],
        compiler_params=pltpu.CompilerParams(vmem_limit_bytes=4 * 1024 * 1024),
    )(*results)
    return (d_tiles, d_gates.T, d_first[None], d_second[None])


def fits(mesh):
    return mesh.shape["space"] == 2 and mesh.shape["expert"] == 16


def solution(mesh):
    in_specs = (
        P(("space", "expert"), None),
        P(("space", "expert"), None),
        P(("space", "expert")),
        P(("space", "expert"), None),
        P(("space", "expert"), None),
        P("expert", None, "space"),
        P("expert", "space", None),
    )
    out_specs = (
        P(("space", "expert"), None),
        P(("space", "expert"), None),
        P("expert", None, "space"),
        P("expert", "space", None),
    )
    return jax.shard_map(
        on_device_fused if fits(mesh) else on_device, mesh=mesh, in_specs=in_specs, out_specs=out_specs, check_vma=False
    )
```

```python
import contextlib
import math

import jax
import jax.numpy as jnp
from jax import lax
from jax.experimental import pallas as pl
from jax.experimental.pallas import tpu as pltpu
from jax.sharding import PartitionSpec as P


def rotation_tables(frames, half_width):
    pair_index = jnp.arange(half_width, dtype=jnp.int32)
    frequency = (1 + pair_index % 3).astype(jnp.float32)
    angles = frames.astype(jnp.float32)[:, None] * frequency[None, :] * (math.pi / 3.0)
    return (jnp.cos(angles), jnp.sin(angles))


def turn_forward(values, cos_table, sin_table):
    half_width = cos_table.shape[1]
    first_half = values[:, :half_width].astype(jnp.float32)
    second_half = values[:, half_width:].astype(jnp.float32)
    return jnp.concatenate(
        [
            cos_table * first_half - sin_table * second_half,
            sin_table * first_half + cos_table * second_half,
        ],
        axis=1,
    )


def turn_back(values, cos_table, sin_table):
    half_width = cos_table.shape[1]
    first_half = values[:, :half_width]
    second_half = values[:, half_width:]
    return jnp.concatenate(
        [
            cos_table * first_half + sin_table * second_half,
            cos_table * second_half - sin_table * first_half,
        ],
        axis=1,
    )


def gelu_pair(hidden):
    gelu_scale = math.sqrt(2.0 / math.pi)
    inner_arg = gelu_scale * (hidden + 0.044715 * hidden * hidden * hidden)
    tangent_h = jnp.tanh(inner_arg)
    activated = 0.5 * hidden * (1.0 + tangent_h)
    slope_term = 0.5 * (1.0 + tangent_h) + 0.5 * hidden * (
        1.0 - tangent_h * tangent_h
    ) * gelu_scale * (1.0 + 0.134145 * hidden * hidden)
    return (activated, slope_term)


def slot_targets(route_ids, capacity, expert_count):
    flat_ids = route_ids.reshape(-1)
    onehot = (flat_ids[:, None] == jnp.arange(expert_count, dtype=jnp.int32)[None, :]).astype(
        jnp.int32
    )
    slot_rank = jnp.sum(jnp.cumsum(onehot, axis=0) * onehot, axis=1) - 1
    return flat_ids * capacity + slot_rank


def fill_buffer(rows_x, rows_dy, gate_rows, targets, slots_total):
    positions = jnp.arange(slots_total, dtype=jnp.int32)
    matches = (positions[:, None] == targets[None, :]).astype(jnp.int32)
    filled = jnp.sum(matches, axis=1)
    source = jnp.sum(matches * jnp.arange(targets.shape[0], dtype=jnp.int32)[None, :], axis=1)
    token_index = source // 2
    occupied = filled > 0
    nothing = jnp.zeros((), jnp.bfloat16)
    buffer_x = jnp.where(occupied[:, None], jnp.take(rows_x, token_index, axis=0), nothing)
    buffer_dy = jnp.where(occupied[:, None], jnp.take(rows_dy, token_index, axis=0), nothing)
    buffer_g = jnp.where(occupied, jnp.take(gate_rows.reshape(-1), source, axis=0), nothing)
    return (buffer_x, buffer_dy, buffer_g)


def block_terms(rows_x, rows_dy, rows_g, first_weight, second_weight):
    hidden = jnp.dot(rows_x, first_weight, preferred_element_type=jnp.float32)
    activated, slope_term = gelu_pair(hidden)
    active = activated.astype(jnp.bfloat16)
    back = jnp.einsum("rd,fd->rf", rows_dy, second_weight, preferred_element_type=jnp.float32)
    gate_part = jnp.sum(back * active.astype(jnp.float32), axis=1)
    gate_col = rows_g.astype(jnp.float32)[:, None]
    scaled = (gate_col * rows_dy.astype(jnp.float32)).astype(jnp.bfloat16)
    pre = (gate_col * back * slope_term).astype(jnp.bfloat16)
    d_first = jnp.einsum("rd,rf->df", rows_x, pre, preferred_element_type=jnp.float32)
    d_second = jnp.einsum("rf,rd->fd", active, scaled, preferred_element_type=jnp.float32)
    row_part = jnp.einsum("rf,df->rd", pre, first_weight, preferred_element_type=jnp.float32)
    return (d_first, d_second, row_part, gate_part)


def run_blocks(blocks_x, blocks_dy, blocks_g, first_weight, second_weight):
    feature_dim = blocks_x.shape[2]

    def scan_step(carried, block_items):
        d_first, d_second, row_part, gate_part = block_terms(
            block_items[0], block_items[1], block_items[2], first_weight, second_weight
        )
        return ((carried[0] + d_first, carried[1] + d_second), (row_part, gate_part))

    start_value = (
        jnp.zeros(first_weight.shape, jnp.float32),
        jnp.zeros(second_weight.shape, jnp.float32),
    )
    sums, stacked = lax.scan(scan_step, start_value, (blocks_x, blocks_dy, blocks_g))
    return (sums[0], sums[1], stacked[0].reshape(-1, feature_dim), stacked[1].reshape(-1))


def on_device(vertex_tiles, cotangent, frames, expert_ids, gate_values, w_in, w_out):
    tile_count = vertex_tiles.shape[0]
    feature_dim = vertex_tiles.shape[1]
    expert_count = lax.axis_size("expert")
    space_count = lax.axis_size("space")
    capacity = 5 * tile_count // (2 * expert_count)
    slots_total = expert_count * capacity
    cos_table, sin_table = rotation_tables(frames, feature_dim // 2)
    rotated = turn_forward(vertex_tiles, cos_table, sin_table).astype(jnp.bfloat16)
    turned = turn_forward(cotangent, cos_table, sin_table).astype(jnp.bfloat16)
    first_weight = w_in[0]
    second_weight = w_out[0]
    own_targets = slot_targets(expert_ids, capacity, expert_count)
    group_x, group_dy, group_g = (
        lax.all_gather(rotated, "space", axis=0, tiled=True),
        lax.all_gather(turned, "space", axis=0, tiled=True),
        lax.all_gather(gate_values, "space", axis=0, tiled=True),
    )
    group_ids = lax.all_gather(expert_ids, "space", axis=0, tiled=True)

    def fill_group(rows_x, rows_dy, gate_rows, route_ids):
        return fill_buffer(
            rows_x, rows_dy, gate_rows, slot_targets(route_ids, capacity, expert_count), slots_total
        )

    buffer_x, buffer_dy, buffer_g = jax.vmap(fill_group)(
        group_x.reshape(space_count, tile_count, feature_dim),
        group_dy.reshape(space_count, tile_count, feature_dim),
        group_g.reshape(space_count, tile_count, 2),
        group_ids.reshape(space_count, tile_count, 2),
    )
    recv_x, recv_dy, recv_g = (
        lax.all_to_all(
            buffer_x.reshape(space_count, expert_count, capacity, feature_dim),
            "expert",
            split_axis=1,
            concat_axis=1,
            tiled=True,
        ),
        lax.all_to_all(
            buffer_dy.reshape(space_count, expert_count, capacity, feature_dim),
            "expert",
            split_axis=1,
            concat_axis=1,
            tiled=True,
        ),
        lax.all_to_all(
            buffer_g.reshape(space_count, expert_count, capacity),
            "expert",
            split_axis=1,
            concat_axis=1,
            tiled=True,
        ),
    )
    d_first, d_second, row_parts, gate_parts = run_blocks(
        recv_x.reshape(space_count, slots_total, feature_dim),
        recv_dy.reshape(space_count, slots_total, feature_dim),
        recv_g.reshape(space_count, slots_total),
        first_weight,
        second_weight,
    )
    summed_rows, summed_gates = (
        lax.psum_scatter(
            row_parts.astype(jnp.bfloat16), "space", scatter_dimension=0, tiled=True
        ).astype(jnp.float32),
        lax.psum_scatter(
            gate_parts.astype(jnp.bfloat16), "space", scatter_dimension=0, tiled=True
        ).astype(jnp.float32),
    )
    back_rows = summed_rows.astype(jnp.bfloat16).reshape(expert_count, capacity, feature_dim)
    back_gates = summed_gates.astype(jnp.bfloat16).reshape(expert_count, capacity)
    home_rows, home_gates = (
        lax.all_to_all(back_rows, "expert", split_axis=0, concat_axis=0, tiled=True),
        lax.all_to_all(back_gates, "expert", split_axis=0, concat_axis=0, tiled=True),
    )
    picked = jnp.take(home_rows.reshape(slots_total, feature_dim), own_targets, axis=0).astype(
        jnp.float32
    )
    picked = picked.reshape(tile_count, 2, feature_dim)
    total = picked[:, 0, :] + picked[:, 1, :]
    d_tiles = turn_back(total, cos_table, sin_table).astype(jnp.bfloat16)
    d_gates = jnp.take(home_gates.reshape(slots_total), own_targets, axis=0).reshape(tile_count, 2)
    return (d_tiles, d_gates, d_first[None], d_second[None])


MESH = pl.DeviceIdType.MESH
BF = jnp.bfloat16
F32 = jnp.float32
LEAD = 16
REST = 4
SELF = 12
CHUNKS = ((0, 4), (4, 8), (8, 12), (12, 16))
DIRECT = 8
SENDS = (13, 14, 15, 0, 1, 2, 3, 4, 5, 6, 7, 8, 9, 10, 11)
FIRST = (13, 14, 0, 1, 2, 3, 15, 4)
DURING = ((6, 5, 7), (8, 9, 10, 11), (), ())


def mark(name):
    return contextlib.nullcontext()


def mm(a, b, ca, cb):
    return lax.dot_general(a, b, (((ca,), (cb,)), ((), ())), preferred_element_type=F32)


def iota(shape, axis):
    return lax.broadcasted_iota(jnp.int32, shape, axis)


def by_quarter(quarter, pieces):
    low = jnp.where(quarter == 0, pieces[0], pieces[1])
    high = jnp.where(quarter == 2, pieces[2], pieces[3])
    return jnp.where(quarter < 2, low, high)


def fused(
    tiles_h, cotan_h, frames_h, ids_h, gates_h, w_in, w_out,
    d_tiles, d_gates, d_first, d_second,
    x_all, sc_all, act_all, pre_all,
    own_gate, far_gate, near_gate, out_gate, home_gate,
    send, recv, own_piece, far_piece, near_in, home_out, home, pick_m, pick_t, rows_acc,
    w1, w2, tiles, cotan, frames_t, ids_t, gates_t,
    sem_w, sem_self, s1, r1, s2, r2, s3, r3, s4, r4, s5, r5, s6, r6,
):
    space = lax.axis_index("space")
    me = lax.axis_index("expert")
    zed, low = me // 4, me % 4
    slots = lax.axis_size("expert")
    other = 1 - space
    count, width = tiles_h.shape
    half = width // 2
    quarter_w = width // 4
    hidden_n = w1.shape[1]

    def flip(value, bits):
        if bits == 1:
            return value + 1 - 2 * lax.rem(value, 2)
        return (value, value, lax.rem(value + 2, 4), 3 - value)[bits]

    def peer(s):
        if s >= SELF:
            return flip(zed, 0) * 4 + flip(low, s - SELF)
        return flip(zed, (1, 3, 2)[s % 3]) * 4 + flip(low, s // 3)

    load1 = pltpu.make_async_copy(w_in.at[0], w1, sem_w.at[0])
    load2 = pltpu.make_async_copy(w_out.at[0], w2, sem_w.at[1])
    small = [
        pltpu.make_async_copy(src, dst, sem_w.at[2 + n])
        for n, (src, dst) in enumerate(
            (
                (ids_h, ids_t), (frames_h, frames_t), (gates_h, gates_t),
                (tiles_h, tiles), (cotan_h, cotan),
            )
        )
    ]
    for copy in small:
        copy.start()

    barrier = pltpu.get_barrier_semaphore()
    peers = [s for s in range(slots) if s != SELF]
    for s in peers:
        pl.semaphore_signal(barrier, inc=1, device_id=(space, peer(s)), device_id_type=MESH)
    for s in range(DIRECT, slots):
        pl.semaphore_signal(
            barrier, inc=1, device_id=(other, peer(s)), device_id_type=MESH
        )

    load1.start()
    load2.start()
    with mark("small"):
        for copy in small:
            copy.wait()
    ids = ids_t[...]
    rel = ids ^ me
    near, plane = rel & 3, (rel >> 2) ^ (rel >> 3)
    rel = jnp.where(plane == 0, SELF + near, 3 * near + plane - 1)
    upper = (iota((count, count), 0) < iota((count, count), 1)).astype(BF)
    hits = [(iota((slots, count), 0) == rel[k : k + 1, :]).astype(F32) for k in range(2)]
    before = mm(jnp.concatenate(hits, axis=0).astype(BF), upper, 1, 0)
    first_total = jnp.sum(hits[0], axis=1, keepdims=True)
    before = (before[:slots], before[slots:] + first_total)
    rows = slots * LEAD
    row_id = iota((rows, count), 0)
    row_tail = (row_id >> 4) * REST + (row_id & 3)
    ranks = []
    for k in range(2):
        rank = jnp.sum(before[k] * hits[k], axis=0, keepdims=True).astype(jnp.int32)
        ranks.append(rank)
        where = rel[k : k + 1, :]
        code_m = jnp.where(rank < LEAD, where * LEAD + rank, -1)
        code_t = jnp.where(rank >= LEAD, where * REST + rank - LEAD, -1)
        pick_m[k] = (row_id == code_m).astype(F32).astype(BF)
        pick_t[k] = (row_tail == code_t).astype(F32).astype(BF)

    diagonal = iota((count, count), 0) == iota((count, count), 1)
    frame = jnp.sum(jnp.where(diagonal, frames_t[...].astype(F32), 0.0), axis=1, keepdims=True)
    frequency = (1 + lax.rem(iota((1, half), 1), 3)).astype(F32)
    sixths = frequency * (frame - 6.0 * jnp.floor(frame * (1.0 / 6.0) + 0.01))
    sixths = sixths - 6.0 * jnp.floor(sixths * (1.0 / 6.0) + 0.01)
    folded = jnp.abs(sixths - 3.0)
    cos_v = jnp.where(
        folded > 2.5, 1.0, jnp.where(folded > 1.5, 0.5, jnp.where(folded > 0.5, -0.5, -1.0))
    )
    side = math.sqrt(3.0) / 2.0
    sin_v = jnp.where(
        (folded > 2.5) | (folded < 0.5), 0.0, jnp.where(sixths < 3.0, side, -side)
    )

    def turn(ref):
        u = ref[:, :half].astype(F32)
        v = ref[:, half:].astype(F32)
        return jnp.concatenate(
            [cos_v * u - sin_v * v, sin_v * u + cos_v * v], axis=1
        ).astype(BF)

    rotated = turn(tiles)
    turned = turn(cotan)
    g0 = gates_t[0:1, :].astype(F32)
    g1 = gates_t[1:2, :].astype(F32)

    def weighed(pick):
        return (pick[0].astype(F32) * g0 + pick[1].astype(F32) * g1).astype(BF)

    quarter = (iota((rows, 1), 0) >> 2) & 3
    send[:, :, 0:width] = (
        mm(pick_m[0] + pick_m[1], rotated, 1, 0).astype(BF).reshape(slots, LEAD, width)
    )
    send[:, :, width : 2 * width] = (
        mm(weighed(pick_m), turned, 1, 0).astype(BF).reshape(slots, LEAD, width)
    )
    tail_x = mm(pick_t[0] + pick_t[1], rotated, 1, 0)
    tail_y = mm(weighed(pick_t), turned, 1, 0)
    send[:, :, 2 * width :] = (
        by_quarter(
            quarter, (tail_x[:, :half], tail_x[:, half:], tail_y[:, :half], tail_y[:, half:])
        )
        .astype(BF)
        .reshape(slots, LEAD, half)
    )
    with mark("barrier_wait"):
        pl.semaphore_wait(barrier, 2 * slots - 1 - DIRECT)

    def remote(src, dst, a, b, who):
        return pltpu.make_async_remote_copy(
            src_ref=src, dst_ref=dst, send_sem=a, recv_sem=b, device_id=who, device_id_type=MESH
        )

    out_copy, relay_copy, piece_copy, home_copy = {}, {}, {}, {}
    piece_gate, home_gates, far_gates = {}, {}, {}
    self_copy = pltpu.make_async_copy(send.at[SELF], recv.at[0, SELF], sem_self)
    self_copy.start()
    relay_copy[SELF] = remote(
        send.at[SELF], recv.at[1, SELF], s2, r2.at[SELF // 4], (other, me)
    )
    relay_copy[SELF].start()
    for s in SENDS:
        out_copy[s] = remote(send.at[s], recv.at[0, s], s1, r1.at[s], (space, peer(s)))
        out_copy[s].start()

    consts = {}
    for lo, hi in CHUNKS:
        block, rest = 2 * (hi - lo) * LEAD, 2 * (hi - lo) * REST
        if block in consts:
            continue
        spread_q = (iota((block, 1), 0) >> 2) & 3
        tall_r = iota((block, rest), 0)
        grow = (tall_r >> 4) * REST + (tall_r & 3) == iota((block, rest), 1)
        flat_c = iota((rest, block), 1)
        same = (flat_c >> 4) * REST + (flat_c & 3) == iota((rest, block), 0)
        pulls = [
            (same & (((flat_c >> 2) & 3) == q)).astype(F32).astype(BF) for q in range(4)
        ]
        consts[block] = (spread_q, grow.astype(F32).astype(BF), pulls)
    gelu_scale = math.sqrt(2.0 / math.pi)
    step_w = 512

    def relay(s):
        with mark("arrive%d" % s):
            out_copy[s].wait_recv()
        relay_copy[s] = remote(
            recv.at[0, s], recv.at[1, s], s2, r2.at[s // 4], (other, me)
        )
        relay_copy[s].start()

    def work(c):
        lo, hi = CHUNKS[c]
        n = hi - lo
        block, rest = 2 * n * LEAD, 2 * n * REST
        chunk = block + rest
        spread_q, grow, pulls = consts[block]
        with mark("relayed%d" % c):
            both = recv.at[0, pl.ds(lo, n)], recv.at[1, pl.ds(lo, n)]
            remote(*both, s2, r2.at[c], (other, me)).wait_recv()
        base = 2 * lo * (LEAD + REST)
        span = slice(lo, hi)
        x_all[base : base + block, :] = recv[:, span, :, 0:width].reshape(block, width)
        sc_all[base : base + block, :] = recv[:, span, :, width : 2 * width].reshape(block, width)
        tail = recv[:, span, :, 2 * width :].reshape(block, half)
        parts = [mm(pull, tail, 1, 0).astype(BF) for pull in pulls]
        x_all[base + block : base + chunk, :] = jnp.concatenate(parts[:2], axis=1)
        sc_all[base + block : base + chunk, :] = jnp.concatenate(parts[2:], axis=1)
        x_c = x_all[base : base + chunk, :]
        y_c = sc_all[base : base + chunk, :]
        acc = rows_acc.at[0:chunk]
        acc[...] = jnp.zeros((chunk, width), F32)

        def tile(f, gate):
            cols = pl.ds(f * step_w, step_w)
            w_a = w1[:, cols]
            h = mm(x_c, w_a, 1, 0)
            back = mm(y_c, w2[cols, :], 1, 1)
            sq = h * h
            t = jnp.tanh(gelu_scale * (h + 0.044715 * h * sq))
            up = 0.5 * (1.0 + t)
            active = (h * up).astype(BF)
            slope = up + 0.5 * h * (1.0 - t * t) * (gelu_scale + (gelu_scale * 0.134145) * sq)
            pre = (back * slope).astype(BF)
            act_all[base : base + chunk, cols] = active
            pre_all[base : base + chunk, cols] = pre
            acc[...] += mm(pre, w_a, 1, 1)
            return gate + jnp.sum(back * active.astype(F32), axis=1, keepdims=True)

        gate = jnp.zeros((chunk, 1), F32)
        for f in range(hidden_n // step_w):
            gate = tile(f, gate)
            for s in DURING[c][f : f + 1] if f < hidden_n // step_w - 1 else DURING[c][f:]:
                relay(s)
        main = rows_acc[0:block, :].astype(BF)
        wide = mm(grow, rows_acc[block:chunk, :].astype(BF), 1, 0)
        packed = by_quarter(
            spread_q, [wide[:, q * quarter_w : (q + 1) * quarter_w] for q in range(4)]
        ).astype(BF)
        gate_b = jnp.broadcast_to(gate.astype(BF).astype(F32), (chunk, 128))
        lane = iota((block, 128), 1)
        gate_m = jnp.where(lane == (iota((block, 128), 0) & (LEAD - 1)), gate_b[:block], 0.0)
        lane = iota((rest, 128), 1)
        gate_r = jnp.where(
            lane == LEAD + (iota((rest, 128), 0) & (REST - 1)), gate_b[block:], 0.0
        )
        gates = jnp.sum(gate_m.reshape(2 * n, LEAD, 128), axis=1) + jnp.sum(
            gate_r.reshape(2 * n, REST, 128), axis=1
        )
        for i in range(n):
            own_gate[lo + i] = gates[i : i + 1]
            far_gate[lo + i] = gates[n + i : n + i + 1]
        both = jnp.concatenate([main, packed], axis=1).reshape(2, n, LEAD, -1)
        far_piece[span] = both[1]
        own_piece[span] = both[0]
        if lo >= DIRECT:
            for s in range(lo, hi):
                there, here = (other, peer(s)), (space, peer(s))
                piece_copy[s] = remote(far_piece.at[s], near_in.at[s], s3, r3.at[2], there)
                piece_copy[s].start()
                far_gates[s] = remote(far_gate.at[s], near_gate.at[s], s5, r5.at[2], there)
                far_gates[s].start()
                if s == SELF:
                    home[s] = own_piece[s]
                    home_gate[s] = own_gate[s]
                    continue
                home_copy[s] = remote(own_piece.at[s], home.at[s], s4, r4, here)
                home_copy[s].start()
                home_gates[s] = remote(own_gate.at[s], home_gate.at[s], s6, r6, here)
                home_gates[s].start()
            return
        piece_gate[c] = remote(
            far_gate.at[pl.ds(lo, n)], near_gate.at[pl.ds(lo, n)],
            s5, r5.at[c], (other, me),
        )
        piece_gate[c].start()
        for s in range(lo, hi):
            piece_copy[s] = remote(
                far_piece.at[s], near_in.at[s], s3, r3.at[c], (other, me)
            )
            piece_copy[s].start()

    def finish(c):
        piece_gate[c].wait_recv()
        span = pl.ds(CHUNKS[c][0], CHUNKS[c][1] - CHUNKS[c][0])
        remote(far_piece.at[span], near_in.at[span], s3, r3.at[c], (other, me)).wait_recv()
        for s in range(*CHUNKS[c]):
            summed = (own_piece[s].astype(F32) + near_in[s].astype(F32)).astype(BF)
            gate = (own_gate[s] + near_gate[s]).astype(BF).astype(F32)
            out_gate[s] = gate
            home_gates[s] = remote(
                out_gate.at[s], home_gate.at[s], s6, r6, (space, peer(s))
            )
            home_gates[s].start()
            home_out[s] = summed
            home_copy[s] = remote(
                home_out.at[s], home.at[s], s4, r4, (space, peer(s))
            )
            home_copy[s].start()

    grad_w = 1024

    def first_tile(f, carry):
        cols = pl.ds(pl.multiple_of(f * grad_w, grad_w), grad_w)
        d_first[:, cols] = mm(x_all[...], pre_all[:, cols], 0, 0)
        return carry

    def second_tile(f, carry):
        cols = pl.ds(pl.multiple_of(f * grad_w, grad_w), grad_w)
        d_second[cols, :] = mm(act_all[:, cols], sc_all[...], 0, 0)
        return carry

    for s in FIRST:
        relay(s)
    self_copy.wait()
    load1.wait()
    load2.wait()
    for c in range(len(CHUNKS)):
        with mark("work%d" % c):
            work(c)
        if 0 < c and CHUNKS[c - 1][0] < DIRECT:
            with mark("finish%d" % (c - 1)):
                finish(c - 1)
    with mark("first"):
        lax.fori_loop(0, hidden_n // grad_w, first_tile, 0)
    with mark("second"):
        lax.fori_loop(0, hidden_n // grad_w, second_tile, 0)
    most, far = pl.ds(0, slots - 1), pl.ds(DIRECT, slots - DIRECT)
    homes = remote(home_out.at[most], home.at[most], s4, r4, (other, me))
    gates = remote(out_gate.at[most], home_gate.at[most], s6, r6, (other, me))
    with mark("homewait"):
        homes.wait_recv()
        gates.wait_recv()
        remote(far_piece.at[far], near_in.at[far], s3, r3.at[2], (other, me)).wait_recv()
        remote(far_gate.at[far], near_gate.at[far], s5, r5.at[2], (other, me)).wait_recv()
    ends = slice(DIRECT, slots)
    home[ends] = (home[ends].astype(F32) + near_in[ends].astype(F32)).astype(BF)
    home_gate[ends] = (home_gate[ends] + near_gate[ends]).astype(BF).astype(F32)

    lead = home[:, :, 0:width].reshape(rows, width)
    packed = home[:, :, width : width + quarter_w].reshape(rows, quarter_w)
    nothing = jnp.zeros((), BF)
    spread = jnp.concatenate([jnp.where(quarter == q, packed, nothing) for q in range(4)], axis=1)
    total = mm(pick_m[0] + pick_m[1], lead, 0, 0) + mm(pick_t[0] + pick_t[1], spread, 0, 0)
    a, b = total[:, :half], total[:, half:]
    d_tiles[...] = jnp.concatenate(
        [cos_v * a + sin_v * b, cos_v * b - sin_v * a], axis=1
    ).astype(BF)
    gate_rows = home_gate[...].reshape(slots, 128).astype(BF)
    for k in range(2):
        got = mm(gate_rows, hits[k].astype(BF), 0, 0)
        row = jnp.sum(jnp.where(iota((128, count), 0) == ranks[k], got, 0.0), axis=0, keepdims=True)
        d_gates[k : k + 1, :] = (row / gates_t[k : k + 1, :].astype(F32)).astype(BF)

    with mark("sendwait"):
        remote(send.at[most], recv.at[0, most], s1, r1.at[0], (other, me)).wait_send()
        remote(recv.at[0], recv.at[1], s2, r2.at[0], (other, me)).wait_send()
        remote(far_piece, near_in, s3, r3.at[0], (other, me)).wait_send()
        remote(far_gate, near_gate, s5, r5.at[0], (other, me)).wait_send()
        homes.wait_send()
        gates.wait_send()


def write_out(*refs):
    held, outs, sem = refs[:4], refs[4:8], refs[8]
    copies = [pltpu.make_async_copy(held[n], outs[n], sem.at[n]) for n in range(4)]
    for copy in copies:
        copy.start()
    for copy in copies:
        copy.wait()


def on_device_fused(vertex_tiles, cotangent, frames, expert_ids, gate_values, w_in, w_out):
    count, width = vertex_tiles.shape
    hidden_n = w_in.shape[2]
    slots = lax.axis_size("expert")
    rows = 2 * slots * (LEAD + REST)
    most = max(hi - lo for lo, hi in CHUNKS)
    block_w = 2 * width + width // 2
    piece_w = width + width // 4
    vmem = pl.BlockSpec(memory_space=pltpu.VMEM)
    hbm = pl.BlockSpec(memory_space=pltpu.HBM)
    dma = pltpu.SemaphoreType.DMA
    shape = jax.ShapeDtypeStruct
    row = pltpu.VMEM((slots, 1, 128), F32)
    d_tiles, d_gates, d_first, d_second = pl.pallas_call(
        fused,
        out_shape=(
            shape((count, width), BF),
            shape((2, count), BF),
            shape((width, hidden_n), F32),
            shape((hidden_n, width), F32),
        ),
        in_specs=[hbm] * 7,
        out_specs=[vmem] * 4,
        scratch_shapes=[
            pltpu.VMEM((rows, width), BF),
            pltpu.VMEM((rows, width), BF),
            pltpu.VMEM((rows, hidden_n), BF),
            pltpu.VMEM((rows, hidden_n), BF),
            row, row, row, row, row,
            pltpu.VMEM((slots, LEAD, block_w), BF),
            pltpu.VMEM((2, slots, LEAD, block_w), BF),
            pltpu.VMEM((slots, LEAD, piece_w), BF),
            pltpu.VMEM((slots, LEAD, piece_w), BF),
            pltpu.VMEM((slots, LEAD, piece_w), BF),
            pltpu.VMEM((slots, LEAD, piece_w), BF),
            pltpu.VMEM((slots, LEAD, piece_w), BF),
            pltpu.VMEM((2, slots * LEAD, count), BF),
            pltpu.VMEM((2, slots * LEAD, count), BF),
            pltpu.VMEM((2 * most * (LEAD + REST), width), F32),
            pltpu.VMEM((width, hidden_n), BF),
            pltpu.VMEM((hidden_n, width), BF),
            pltpu.VMEM((count, width), BF),
            pltpu.VMEM((count, width), BF),
            pltpu.VMEM((1, count), jnp.int32),
            pltpu.VMEM((2, count), jnp.int32),
            pltpu.VMEM((2, count), BF),
            dma((7,)),
            dma(()),
        ]
        + [dma(()), dma((slots,)), dma(()), dma((4,)), dma(()), dma((3,)), dma(()), dma(())]
        + [dma(()), dma((3,)), dma(()), dma(())],
        compiler_params=pltpu.CompilerParams(
            collective_id=0, has_side_effects=True, vmem_limit_bytes=36 * 1024 * 1024
        ),
    )(
        *[
            pltpu.with_memory_space_constraint(a, pltpu.HBM)
            for a in (
                vertex_tiles, cotangent, frames[None], expert_ids.T, gate_values.T, w_in, w_out
            )
        ]
    )
    results = (d_tiles, d_gates, d_first, d_second)
    d_tiles, d_gates, d_first, d_second = pl.pallas_call(
        write_out,
        out_shape=tuple(shape(a.shape, a.dtype) for a in results),
        in_specs=[vmem] * 4,
        out_specs=[hbm] * 4,
        scratch_shapes=[dma((4,))],
        compiler_params=pltpu.CompilerParams(vmem_limit_bytes=4 * 1024 * 1024),
    )(*results)
    return (d_tiles, d_gates.T, d_first[None], d_second[None])


def fits(mesh):
    return mesh.shape["space"] == 2 and mesh.shape["expert"] == 16


def solution(mesh):
    in_specs = (
        P(("space", "expert"), None),
        P(("space", "expert"), None),
        P(("space", "expert")),
        P(("space", "expert"), None),
        P(("space", "expert"), None),
        P("expert", None, "space"),
        P("expert", "space", None),
    )
    out_specs = (
        P(("space", "expert"), None),
        P(("space", "expert"), None),
        P("expert", None, "space"),
        P("expert", "space", None),
    )
    return jax.shard_map(
        on_device_fused if fits(mesh) else on_device, mesh=mesh, in_specs=in_specs, out_specs=out_specs, check_vma=False
    )
```

```python
import contextlib
import math

import jax
import jax.numpy as jnp
from jax import lax
from jax.experimental import pallas as pl
from jax.experimental.pallas import tpu as pltpu
from jax.sharding import PartitionSpec as P


def rotation_tables(frames, half_width):
    pair_index = jnp.arange(half_width, dtype=jnp.int32)
    frequency = (1 + pair_index % 3).astype(jnp.float32)
    angles = frames.astype(jnp.float32)[:, None] * frequency[None, :] * (math.pi / 3.0)
    return (jnp.cos(angles), jnp.sin(angles))


def turn_forward(values, cos_table, sin_table):
    half_width = cos_table.shape[1]
    first_half = values[:, :half_width].astype(jnp.float32)
    second_half = values[:, half_width:].astype(jnp.float32)
    return jnp.concatenate(
        [
            cos_table * first_half - sin_table * second_half,
            sin_table * first_half + cos_table * second_half,
        ],
        axis=1,
    )


def turn_back(values, cos_table, sin_table):
    half_width = cos_table.shape[1]
    first_half = values[:, :half_width]
    second_half = values[:, half_width:]
    return jnp.concatenate(
        [
            cos_table * first_half + sin_table * second_half,
            cos_table * second_half - sin_table * first_half,
        ],
        axis=1,
    )


def gelu_pair(hidden):
    gelu_scale = math.sqrt(2.0 / math.pi)
    inner_arg = gelu_scale * (hidden + 0.044715 * hidden * hidden * hidden)
    tangent_h = jnp.tanh(inner_arg)
    activated = 0.5 * hidden * (1.0 + tangent_h)
    slope_term = 0.5 * (1.0 + tangent_h) + 0.5 * hidden * (
        1.0 - tangent_h * tangent_h
    ) * gelu_scale * (1.0 + 0.134145 * hidden * hidden)
    return (activated, slope_term)


def slot_targets(route_ids, capacity, expert_count):
    flat_ids = route_ids.reshape(-1)
    onehot = (flat_ids[:, None] == jnp.arange(expert_count, dtype=jnp.int32)[None, :]).astype(
        jnp.int32
    )
    slot_rank = jnp.sum(jnp.cumsum(onehot, axis=0) * onehot, axis=1) - 1
    return flat_ids * capacity + slot_rank


def fill_buffer(rows_x, rows_dy, gate_rows, targets, slots_total):
    positions = jnp.arange(slots_total, dtype=jnp.int32)
    matches = (positions[:, None] == targets[None, :]).astype(jnp.int32)
    filled = jnp.sum(matches, axis=1)
    source = jnp.sum(matches * jnp.arange(targets.shape[0], dtype=jnp.int32)[None, :], axis=1)
    token_index = source // 2
    occupied = filled > 0
    nothing = jnp.zeros((), jnp.bfloat16)
    buffer_x = jnp.where(occupied[:, None], jnp.take(rows_x, token_index, axis=0), nothing)
    buffer_dy = jnp.where(occupied[:, None], jnp.take(rows_dy, token_index, axis=0), nothing)
    buffer_g = jnp.where(occupied, jnp.take(gate_rows.reshape(-1), source, axis=0), nothing)
    return (buffer_x, buffer_dy, buffer_g)


def block_terms(rows_x, rows_dy, rows_g, first_weight, second_weight):
    hidden = jnp.dot(rows_x, first_weight, preferred_element_type=jnp.float32)
    activated, slope_term = gelu_pair(hidden)
    active = activated.astype(jnp.bfloat16)
    back = jnp.einsum("rd,fd->rf", rows_dy, second_weight, preferred_element_type=jnp.float32)
    gate_part = jnp.sum(back * active.astype(jnp.float32), axis=1)
    gate_col = rows_g.astype(jnp.float32)[:, None]
    scaled = (gate_col * rows_dy.astype(jnp.float32)).astype(jnp.bfloat16)
    pre = (gate_col * back * slope_term).astype(jnp.bfloat16)
    d_first = jnp.einsum("rd,rf->df", rows_x, pre, preferred_element_type=jnp.float32)
    d_second = jnp.einsum("rf,rd->fd", active, scaled, preferred_element_type=jnp.float32)
    row_part = jnp.einsum("rf,df->rd", pre, first_weight, preferred_element_type=jnp.float32)
    return (d_first, d_second, row_part, gate_part)


def run_blocks(blocks_x, blocks_dy, blocks_g, first_weight, second_weight):
    feature_dim = blocks_x.shape[2]

    def scan_step(carried, block_items):
        d_first, d_second, row_part, gate_part = block_terms(
            block_items[0], block_items[1], block_items[2], first_weight, second_weight
        )
        return ((carried[0] + d_first, carried[1] + d_second), (row_part, gate_part))

    start_value = (
        jnp.zeros(first_weight.shape, jnp.float32),
        jnp.zeros(second_weight.shape, jnp.float32),
    )
    sums, stacked = lax.scan(scan_step, start_value, (blocks_x, blocks_dy, blocks_g))
    return (sums[0], sums[1], stacked[0].reshape(-1, feature_dim), stacked[1].reshape(-1))


def on_device(vertex_tiles, cotangent, frames, expert_ids, gate_values, w_in, w_out):
    tile_count = vertex_tiles.shape[0]
    feature_dim = vertex_tiles.shape[1]
    expert_count = lax.axis_size("expert")
    space_count = lax.axis_size("space")
    capacity = 5 * tile_count // (2 * expert_count)
    slots_total = expert_count * capacity
    cos_table, sin_table = rotation_tables(frames, feature_dim // 2)
    rotated = turn_forward(vertex_tiles, cos_table, sin_table).astype(jnp.bfloat16)
    turned = turn_forward(cotangent, cos_table, sin_table).astype(jnp.bfloat16)
    first_weight = w_in[0]
    second_weight = w_out[0]
    own_targets = slot_targets(expert_ids, capacity, expert_count)
    group_x, group_dy, group_g = (
        lax.all_gather(rotated, "space", axis=0, tiled=True),
        lax.all_gather(turned, "space", axis=0, tiled=True),
        lax.all_gather(gate_values, "space", axis=0, tiled=True),
    )
    group_ids = lax.all_gather(expert_ids, "space", axis=0, tiled=True)

    def fill_group(rows_x, rows_dy, gate_rows, route_ids):
        return fill_buffer(
            rows_x, rows_dy, gate_rows, slot_targets(route_ids, capacity, expert_count), slots_total
        )

    buffer_x, buffer_dy, buffer_g = jax.vmap(fill_group)(
        group_x.reshape(space_count, tile_count, feature_dim),
        group_dy.reshape(space_count, tile_count, feature_dim),
        group_g.reshape(space_count, tile_count, 2),
        group_ids.reshape(space_count, tile_count, 2),
    )
    recv_x, recv_dy, recv_g = (
        lax.all_to_all(
            buffer_x.reshape(space_count, expert_count, capacity, feature_dim),
            "expert",
            split_axis=1,
            concat_axis=1,
            tiled=True,
        ),
        lax.all_to_all(
            buffer_dy.reshape(space_count, expert_count, capacity, feature_dim),
            "expert",
            split_axis=1,
            concat_axis=1,
            tiled=True,
        ),
        lax.all_to_all(
            buffer_g.reshape(space_count, expert_count, capacity),
            "expert",
            split_axis=1,
            concat_axis=1,
            tiled=True,
        ),
    )
    d_first, d_second, row_parts, gate_parts = run_blocks(
        recv_x.reshape(space_count, slots_total, feature_dim),
        recv_dy.reshape(space_count, slots_total, feature_dim),
        recv_g.reshape(space_count, slots_total),
        first_weight,
        second_weight,
    )
    summed_rows, summed_gates = (
        lax.psum_scatter(
            row_parts.astype(jnp.bfloat16), "space", scatter_dimension=0, tiled=True
        ).astype(jnp.float32),
        lax.psum_scatter(
            gate_parts.astype(jnp.bfloat16), "space", scatter_dimension=0, tiled=True
        ).astype(jnp.float32),
    )
    back_rows = summed_rows.astype(jnp.bfloat16).reshape(expert_count, capacity, feature_dim)
    back_gates = summed_gates.astype(jnp.bfloat16).reshape(expert_count, capacity)
    home_rows, home_gates = (
        lax.all_to_all(back_rows, "expert", split_axis=0, concat_axis=0, tiled=True),
        lax.all_to_all(back_gates, "expert", split_axis=0, concat_axis=0, tiled=True),
    )
    picked = jnp.take(home_rows.reshape(slots_total, feature_dim), own_targets, axis=0).astype(
        jnp.float32
    )
    picked = picked.reshape(tile_count, 2, feature_dim)
    total = picked[:, 0, :] + picked[:, 1, :]
    d_tiles = turn_back(total, cos_table, sin_table).astype(jnp.bfloat16)
    d_gates = jnp.take(home_gates.reshape(slots_total), own_targets, axis=0).reshape(tile_count, 2)
    return (d_tiles, d_gates, d_first[None], d_second[None])


MESH = pl.DeviceIdType.MESH
BF = jnp.bfloat16
F32 = jnp.float32
LEAD = 16
REST = 4
SELF = 12
CHUNKS = ((0, 4), (4, 8), (8, 12), (12, 16))
DIRECT = 8
PARTS = 4
SENDS = (13, 14, 15, 0, 1, 2, 3, 4, 5, 6, 7, 8, 9, 10, 11)
FIRST = (13, 14, 0, 1, 2, 3, 15, 4)
DURING = ((6, 5, 7), (8, 9, 10, 11), (), ())


def mark(name):
    return contextlib.nullcontext()


def mm(a, b, ca, cb):
    return lax.dot_general(a, b, (((ca,), (cb,)), ((), ())), preferred_element_type=F32)


def iota(shape, axis):
    return lax.broadcasted_iota(jnp.int32, shape, axis)


def by_quarter(quarter, pieces):
    low = jnp.where(quarter == 0, pieces[0], pieces[1])
    high = jnp.where(quarter == 2, pieces[2], pieces[3])
    return jnp.where(quarter < 2, low, high)


def fused(
    tiles_h, cotan_h, frames_h, ids_h, gates_h, w_in, w_out,
    d_tiles, d_gates, d_first, d_second,
    x_all, sc_all, act_all, pre_all,
    own_gate, far_gate, near_gate, out_gate, home_gate,
    send, recv, own_piece, far_piece, near_in, home_out, home, pick_m, pick_t, rows_acc,
    w1, w2, tiles, cotan, frames_t, ids_t, gates_t,
    sem_w, sem_self, s1, r1, s2, r2, s3, r3, s4, r4, s5, r5, s6, r6,
):
    space = lax.axis_index("space")
    me = lax.axis_index("expert")
    zed, low = me // 4, me % 4
    slots = lax.axis_size("expert")
    other = 1 - space
    count, width = tiles_h.shape
    half = width // 2
    quarter_w = width // 4
    hidden_n = w1.shape[1]

    def flip(value, bits):
        if bits == 1:
            return value + 1 - 2 * lax.rem(value, 2)
        return (value, value, lax.rem(value + 2, 4), 3 - value)[bits]

    def peer(s):
        if s >= SELF:
            return flip(zed, 0) * 4 + flip(low, s - SELF)
        return flip(zed, (1, 3, 2)[s % 3]) * 4 + flip(low, s // 3)

    load1 = pltpu.make_async_copy(w_in.at[0], w1, sem_w.at[0])
    load2 = pltpu.make_async_copy(w_out.at[0], w2, sem_w.at[1])
    small = [
        pltpu.make_async_copy(src, dst, sem_w.at[2 + n])
        for n, (src, dst) in enumerate(
            (
                (ids_h, ids_t), (frames_h, frames_t), (gates_h, gates_t),
                (tiles_h, tiles), (cotan_h, cotan),
            )
        )
    ]
    for copy in small:
        copy.start()

    barrier = pltpu.get_barrier_semaphore()
    peers = [s for s in range(slots) if s != SELF]
    for s in peers:
        pl.semaphore_signal(barrier, inc=1, device_id=(space, peer(s)), device_id_type=MESH)
    for s in range(DIRECT, slots):
        pl.semaphore_signal(
            barrier, inc=1, device_id=(other, peer(s)), device_id_type=MESH
        )

    load1.start()
    load2.start()
    small[0].wait()
    ids = ids_t[...]
    rel = ids ^ me
    near, plane = rel & 3, (rel >> 2) ^ (rel >> 3)
    rel = jnp.where(plane == 0, SELF + near, 3 * near + plane - 1)
    upper = (iota((count, count), 0) < iota((count, count), 1)).astype(BF)
    hits = [(iota((slots, count), 0) == rel[k : k + 1, :]).astype(F32) for k in range(2)]
    before = mm(jnp.concatenate(hits, axis=0).astype(BF), upper, 1, 0)
    first_total = jnp.sum(hits[0], axis=1, keepdims=True)
    before = (before[:slots], before[slots:] + first_total)
    rows = slots * LEAD
    row_id = iota((rows, count), 0)
    row_tail = (row_id >> 4) * REST + (row_id & 3)
    ranks = []
    for k in range(2):
        rank = jnp.sum(before[k] * hits[k], axis=0, keepdims=True).astype(jnp.int32)
        ranks.append(rank)
        where = rel[k : k + 1, :]
        code_m = jnp.where(rank < LEAD, where * LEAD + rank, -1)
        code_t = jnp.where(rank >= LEAD, where * REST + rank - LEAD, -1)
        pick_m[k] = (row_id == code_m).astype(F32).astype(BF)
        pick_t[k] = (row_tail == code_t).astype(F32).astype(BF)

    small[1].wait()
    diagonal = iota((count, count), 0) == iota((count, count), 1)
    frame = jnp.sum(jnp.where(diagonal, frames_t[...].astype(F32), 0.0), axis=1, keepdims=True)
    frequency = (1 + lax.rem(iota((1, half), 1), 3)).astype(F32)
    sixths = frequency * (frame - 6.0 * jnp.floor(frame * (1.0 / 6.0) + 0.01))
    sixths = sixths - 6.0 * jnp.floor(sixths * (1.0 / 6.0) + 0.01)
    folded = jnp.abs(sixths - 3.0)
    cos_v = jnp.where(
        folded > 2.5, 1.0, jnp.where(folded > 1.5, 0.5, jnp.where(folded > 0.5, -0.5, -1.0))
    )
    side = math.sqrt(3.0) / 2.0
    sin_v = jnp.where(
        (folded > 2.5) | (folded < 0.5), 0.0, jnp.where(sixths < 3.0, side, -side)
    )

    def turn(ref):
        u = ref[:, :half].astype(F32)
        v = ref[:, half:].astype(F32)
        return jnp.concatenate(
            [cos_v * u - sin_v * v, sin_v * u + cos_v * v], axis=1
        ).astype(BF)

    small[3].wait()
    rotated = turn(tiles)
    small[4].wait()
    turned = turn(cotan)
    small[2].wait()
    g0 = gates_t[0:1, :].astype(F32)
    g1 = gates_t[1:2, :].astype(F32)

    def weighed(pick):
        return (pick[0].astype(F32) * g0 + pick[1].astype(F32) * g1).astype(BF)

    quarter = (iota((rows, 1), 0) >> 2) & 3
    send[:, :, 0:width] = (
        mm(pick_m[0] + pick_m[1], rotated, 1, 0).astype(BF).reshape(slots, LEAD, width)
    )
    send[:, :, width : 2 * width] = (
        mm(weighed(pick_m), turned, 1, 0).astype(BF).reshape(slots, LEAD, width)
    )
    tail_x = mm(pick_t[0] + pick_t[1], rotated, 1, 0)
    tail_y = mm(weighed(pick_t), turned, 1, 0)
    send[:, :, 2 * width :] = (
        by_quarter(
            quarter, (tail_x[:, :half], tail_x[:, half:], tail_y[:, :half], tail_y[:, half:])
        )
        .astype(BF)
        .reshape(slots, LEAD, half)
    )
    with mark("barrier_wait"):
        pl.semaphore_wait(barrier, 2 * slots - 1 - DIRECT)

    def remote(src, dst, a, b, who):
        return pltpu.make_async_remote_copy(
            src_ref=src, dst_ref=dst, send_sem=a, recv_sem=b, device_id=who, device_id_type=MESH
        )

    out_copy, relay_copy, piece_copy, home_copy = {}, {}, {}, {}
    piece_gate, home_gates, far_gates = {}, {}, {}
    self_copy = pltpu.make_async_copy(send.at[SELF], recv.at[0, SELF], sem_self)
    self_copy.start()
    relay_copy[SELF] = remote(
        send.at[SELF], recv.at[1, SELF], s2, r2.at[SELF // 4], (other, me)
    )
    relay_copy[SELF].start()
    for s in SENDS:
        out_copy[s] = remote(send.at[s], recv.at[0, s], s1, r1.at[s], (space, peer(s)))
        out_copy[s].start()

    consts = {}
    for lo, hi in CHUNKS:
        block, rest = 2 * (hi - lo) * LEAD, 2 * (hi - lo) * REST
        if block in consts:
            continue
        spread_q = (iota((block, 1), 0) >> 2) & 3
        tall_r = iota((block, rest), 0)
        grow = (tall_r >> 4) * REST + (tall_r & 3) == iota((block, rest), 1)
        flat_c = iota((rest, block), 1)
        same = (flat_c >> 4) * REST + (flat_c & 3) == iota((rest, block), 0)
        pulls = [
            (same & (((flat_c >> 2) & 3) == q)).astype(F32).astype(BF) for q in range(4)
        ]
        consts[block] = (spread_q, grow.astype(F32).astype(BF), pulls)
    gelu_scale = math.sqrt(2.0 / math.pi)
    step_w = 512

    def relay(s):
        with mark("arrive%d" % s):
            out_copy[s].wait_recv()
        relay_copy[s] = remote(
            recv.at[0, s], recv.at[1, s], s2, r2.at[s // 4], (other, me)
        )
        relay_copy[s].start()

    def work(c):
        lo, hi = CHUNKS[c]
        n = hi - lo
        block, rest = 2 * n * LEAD, 2 * n * REST
        chunk = block + rest
        spread_q, grow, pulls = consts[block]
        with mark("relayed%d" % c):
            both = recv.at[0, pl.ds(lo, n)], recv.at[1, pl.ds(lo, n)]
            remote(*both, s2, r2.at[c], (other, me)).wait_recv()
        base = 2 * lo * (LEAD + REST)
        span = slice(lo, hi)
        x_all[base : base + block, :] = recv[:, span, :, 0:width].reshape(block, width)
        sc_all[base : base + block, :] = recv[:, span, :, width : 2 * width].reshape(block, width)
        tail = recv[:, span, :, 2 * width :].reshape(block, half)
        parts = [mm(pull, tail, 1, 0).astype(BF) for pull in pulls]
        x_all[base + block : base + chunk, :] = jnp.concatenate(parts[:2], axis=1)
        sc_all[base + block : base + chunk, :] = jnp.concatenate(parts[2:], axis=1)
        x_c = x_all[base : base + chunk, :]
        y_c = sc_all[base : base + chunk, :]
        acc = rows_acc.at[0:chunk]
        acc[...] = jnp.zeros((chunk, width), F32)

        def tile(f, gate):
            cols = pl.ds(f * step_w, step_w)
            w_a = w1[:, cols]
            h = mm(x_c, w_a, 1, 0)
            back = mm(y_c, w2[cols, :], 1, 1)
            sq = h * h
            t = jnp.tanh(gelu_scale * (h + 0.044715 * h * sq))
            up = 0.5 * (1.0 + t)
            active = (h * up).astype(BF)
            slope = up + 0.5 * h * (1.0 - t * t) * (gelu_scale + (gelu_scale * 0.134145) * sq)
            pre = (back * slope).astype(BF)
            act_all[base : base + chunk, cols] = active
            pre_all[base : base + chunk, cols] = pre
            acc[...] += mm(pre, w_a, 1, 1)
            return gate + jnp.sum(back * active.astype(F32), axis=1, keepdims=True)

        gate = jnp.zeros((chunk, 1), F32)
        for f in range(hidden_n // step_w):
            gate = tile(f, gate)
            for s in DURING[c][f : f + 1] if f < hidden_n // step_w - 1 else DURING[c][f:]:
                relay(s)
        main = rows_acc[0:block, :].astype(BF)
        wide = mm(grow, rows_acc[block:chunk, :].astype(BF), 1, 0)
        packed = by_quarter(
            spread_q, [wide[:, q * quarter_w : (q + 1) * quarter_w] for q in range(4)]
        ).astype(BF)
        gate_b = jnp.broadcast_to(gate.astype(BF).astype(F32), (chunk, 128))
        lane = iota((block, 128), 1)
        gate_m = jnp.where(lane == (iota((block, 128), 0) & (LEAD - 1)), gate_b[:block], 0.0)
        lane = iota((rest, 128), 1)
        gate_r = jnp.where(
            lane == LEAD + (iota((rest, 128), 0) & (REST - 1)), gate_b[block:], 0.0
        )
        gates = jnp.sum(gate_m.reshape(2 * n, LEAD, 128), axis=1) + jnp.sum(
            gate_r.reshape(2 * n, REST, 128), axis=1
        )
        for i in range(n):
            own_gate[lo + i] = gates[i : i + 1]
            far_gate[lo + i] = gates[n + i : n + i + 1]
        both = jnp.concatenate([main, packed], axis=1).reshape(2, n, LEAD, -1)
        far_piece[span] = both[1]
        own_piece[span] = both[0]
        if lo >= DIRECT:
            for s in range(lo, hi):
                there, here = (other, peer(s)), (space, peer(s))
                piece_copy[s] = remote(far_piece.at[s], near_in.at[s], s3, r3.at[2], there)
                piece_copy[s].start()
                far_gates[s] = remote(far_gate.at[s], near_gate.at[s], s5, r5.at[2], there)
                far_gates[s].start()
                if s == SELF:
                    home[s] = own_piece[s]
                    home_gate[s] = own_gate[s]
                    continue
                home_copy[s] = remote(own_piece.at[s], home.at[s], s4, r4, here)
                home_copy[s].start()
                home_gates[s] = remote(own_gate.at[s], home_gate.at[s], s6, r6, here)
                home_gates[s].start()
            return
        piece_gate[c] = remote(
            far_gate.at[pl.ds(lo, n)], near_gate.at[pl.ds(lo, n)],
            s5, r5.at[c], (other, me),
        )
        piece_gate[c].start()
        for s in range(lo, hi):
            piece_copy[s] = remote(
                far_piece.at[s], near_in.at[s], s3, r3.at[c], (other, me)
            )
            piece_copy[s].start()

    def finish(c):
        piece_gate[c].wait_recv()
        span = pl.ds(CHUNKS[c][0], CHUNKS[c][1] - CHUNKS[c][0])
        remote(far_piece.at[span], near_in.at[span], s3, r3.at[c], (other, me)).wait_recv()
        for s in range(*CHUNKS[c]):
            summed = (own_piece[s].astype(F32) + near_in[s].astype(F32)).astype(BF)
            gate = (own_gate[s] + near_gate[s]).astype(BF).astype(F32)
            out_gate[s] = gate
            home_gates[s] = remote(
                out_gate.at[s], home_gate.at[s], s6, r6, (space, peer(s))
            )
            home_gates[s].start()
            home_out[s] = summed
            home_copy[s] = remote(
                home_out.at[s], home.at[s], s4, r4, (space, peer(s))
            )
            home_copy[s].start()

    grad_w = 1024

    def first_tile(f, carry):
        cols = pl.ds(pl.multiple_of(f * grad_w, grad_w), grad_w)
        d_first[:, cols] = mm(x_all[...], pre_all[:, cols], 0, 0)
        return carry

    def second_tile(f, carry):
        cols = pl.ds(pl.multiple_of(f * grad_w, grad_w), grad_w)
        d_second[cols, :] = mm(act_all[:, cols], sc_all[...], 0, 0)
        return carry

    for s in FIRST:
        relay(s)
    self_copy.wait()
    load1.wait()
    load2.wait()
    for c in range(len(CHUNKS)):
        with mark("work%d" % c):
            work(c)
        if 0 < c and CHUNKS[c - 1][0] < DIRECT:
            with mark("finish%d" % (c - 1)):
                finish(c - 1)
    with mark("first"):
        lax.fori_loop(0, hidden_n // grad_w, first_tile, 0)
    with mark("second"):
        lax.fori_loop(0, hidden_n // grad_w, second_tile, 0)
    most, far = pl.ds(0, slots - 1), pl.ds(DIRECT, slots - DIRECT)
    homes = remote(home_out.at[most], home.at[most], s4, r4, (other, me))
    gates = remote(out_gate.at[most], home_gate.at[most], s6, r6, (other, me))
    with mark("homewait"):
        homes.wait_recv()
        gates.wait_recv()
        remote(far_piece.at[far], near_in.at[far], s3, r3.at[2], (other, me)).wait_recv()
        remote(far_gate.at[far], near_gate.at[far], s5, r5.at[2], (other, me)).wait_recv()
    ends = slice(DIRECT, slots)
    home[ends] = (home[ends].astype(F32) + near_in[ends].astype(F32)).astype(BF)
    home_gate[ends] = (home_gate[ends] + near_gate[ends]).astype(BF).astype(F32)

    lead = home[:, :, 0:width].reshape(rows, width)
    packed = home[:, :, width : width + quarter_w].reshape(rows, quarter_w)
    nothing = jnp.zeros((), BF)
    spread = jnp.concatenate([jnp.where(quarter == q, packed, nothing) for q in range(4)], axis=1)
    total = mm(pick_m[0] + pick_m[1], lead, 0, 0) + mm(pick_t[0] + pick_t[1], spread, 0, 0)
    a, b = total[:, :half], total[:, half:]
    d_tiles[...] = jnp.concatenate(
        [cos_v * a + sin_v * b, cos_v * b - sin_v * a], axis=1
    ).astype(BF)
    gate_rows = home_gate[...].reshape(slots, 128).astype(BF)
    for k in range(2):
        got = mm(gate_rows, hits[k].astype(BF), 0, 0)
        row = jnp.sum(jnp.where(iota((128, count), 0) == ranks[k], got, 0.0), axis=0, keepdims=True)
        d_gates[k : k + 1, :] = (row / gates_t[k : k + 1, :].astype(F32)).astype(BF)

    with mark("sendwait"):
        remote(send.at[most], recv.at[0, most], s1, r1.at[0], (other, me)).wait_send()
        remote(recv.at[0], recv.at[1], s2, r2.at[0], (other, me)).wait_send()
        remote(far_piece, near_in, s3, r3.at[0], (other, me)).wait_send()
        remote(far_gate, near_gate, s5, r5.at[0], (other, me)).wait_send()
        homes.wait_send()
        gates.wait_send()


def write_out(*refs):
    held, outs, sem = refs[:4], refs[4:8], refs[8]
    copies = [pltpu.make_async_copy(held[n], outs[n], sem.at[n]) for n in range(2)]
    for n in (2, 3):
        part = held[n].shape[0] // PARTS
        for p in range(PARTS):
            rows = pl.ds(p * part, part)
            copies.append(
                pltpu.make_async_copy(held[n].at[rows], outs[n].at[rows], sem.at[len(copies)])
            )
    for copy in copies:
        copy.start()
    for copy in copies:
        copy.wait()


def on_device_fused(vertex_tiles, cotangent, frames, expert_ids, gate_values, w_in, w_out):
    count, width = vertex_tiles.shape
    hidden_n = w_in.shape[2]
    slots = lax.axis_size("expert")
    rows = 2 * slots * (LEAD + REST)
    most = max(hi - lo for lo, hi in CHUNKS)
    block_w = 2 * width + width // 2
    piece_w = width + width // 4
    vmem = pl.BlockSpec(memory_space=pltpu.VMEM)
    hbm = pl.BlockSpec(memory_space=pltpu.HBM)
    dma = pltpu.SemaphoreType.DMA
    shape = jax.ShapeDtypeStruct
    row = pltpu.VMEM((slots, 1, 128), F32)
    d_tiles, d_gates, d_first, d_second = pl.pallas_call(
        fused,
        out_shape=(
            shape((count, width), BF),
            shape((2, count), BF),
            shape((width, hidden_n), F32),
            shape((hidden_n, width), F32),
        ),
        in_specs=[hbm] * 7,
        out_specs=[vmem] * 4,
        scratch_shapes=[
            pltpu.VMEM((rows, width), BF),
            pltpu.VMEM((rows, width), BF),
            pltpu.VMEM((rows, hidden_n), BF),
            pltpu.VMEM((rows, hidden_n), BF),
            row, row, row, row, row,
            pltpu.VMEM((slots, LEAD, block_w), BF),
            pltpu.VMEM((2, slots, LEAD, block_w), BF),
            pltpu.VMEM((slots, LEAD, piece_w), BF),
            pltpu.VMEM((slots, LEAD, piece_w), BF),
            pltpu.VMEM((slots, LEAD, piece_w), BF),
            pltpu.VMEM((slots, LEAD, piece_w), BF),
            pltpu.VMEM((slots, LEAD, piece_w), BF),
            pltpu.VMEM((2, slots * LEAD, count), BF),
            pltpu.VMEM((2, slots * LEAD, count), BF),
            pltpu.VMEM((2 * most * (LEAD + REST), width), F32),
            pltpu.VMEM((width, hidden_n), BF),
            pltpu.VMEM((hidden_n, width), BF),
            pltpu.VMEM((count, width), BF),
            pltpu.VMEM((count, width), BF),
            pltpu.VMEM((1, count), jnp.int32),
            pltpu.VMEM((2, count), jnp.int32),
            pltpu.VMEM((2, count), BF),
            dma((7,)),
            dma(()),
        ]
        + [dma(()), dma((slots,)), dma(()), dma((4,)), dma(()), dma((3,)), dma(()), dma(())]
        + [dma(()), dma((3,)), dma(()), dma(())],
        compiler_params=pltpu.CompilerParams(
            collective_id=0, has_side_effects=True, vmem_limit_bytes=36 * 1024 * 1024
        ),
    )(
        *[
            pltpu.with_memory_space_constraint(a, pltpu.HBM)
            for a in (
                vertex_tiles, cotangent, frames[None], expert_ids.T, gate_values.T, w_in, w_out
            )
        ]
    )
    results = (d_tiles, d_gates, d_first, d_second)
    d_tiles, d_gates, d_first, d_second = pl.pallas_call(
        write_out,
        out_shape=tuple(shape(a.shape, a.dtype) for a in results),
        in_specs=[vmem] * 4,
        out_specs=[hbm] * 4,
        scratch_shapes=[dma((2 + 2 * PARTS,))],
        compiler_params=pltpu.CompilerParams(vmem_limit_bytes=4 * 1024 * 1024),
    )(*results)
    return (d_tiles, d_gates.T, d_first[None], d_second[None])


def fits(mesh):
    return mesh.shape["space"] == 2 and mesh.shape["expert"] == 16


def solution(mesh):
    in_specs = (
        P(("space", "expert"), None),
        P(("space", "expert"), None),
        P(("space", "expert")),
        P(("space", "expert"), None),
        P(("space", "expert"), None),
        P("expert", None, "space"),
        P("expert", "space", None),
    )
    out_specs = (
        P(("space", "expert"), None),
        P(("space", "expert"), None),
        P("expert", None, "space"),
        P("expert", "space", None),
    )
    return jax.shard_map(
        on_device_fused if fits(mesh) else on_device, mesh=mesh, in_specs=in_specs, out_specs=out_specs, check_vma=False
    )
```
